32 devices in a mesh: dp: 4 (over x, core), expert: 8 (over z, y).
Axes of the slice: x: 2, y: 2, z: 4, core: 2. Of those that a mesh axis runs over, the one named last changes fastest.
Arguments:
- dense_weights: bfloat16 [3, 5632, 2048], P(None, 'dp', 'expert'), may hold values from -0.125 to 0.125
- tokens: bfloat16 [1024, 2048], P('expert'), may hold values from -6 to 6
- cotangent: bfloat16 [1024, 2048], P('expert'), may hold values from -6 to 6
- routes: int32 [1024, 4], P('expert'), may hold values from 0 to 7, all different within a row; in each aligned block of 128 rows (0 to 127, 128 to 255, ...) at most 80 rows name the same one
- route_gates: float32 [1024, 4], P('expert'), may hold values from 0.2 to 1
- unit_perm: int32 [2, 5632], replicated, may hold values from 0 to 5631, as said below
- slab_owner: int32 [8], replicated, may hold values from 0 to 7, each once
Outputs:
- mixed: bfloat16 [1024, 2048], P('expert', 'dp')
- token_grad: bfloat16 [1024, 2048], P('expert', 'dp')
- expert_grad: bfloat16 [8, 3, 1408, 2048], P('expert', None, 'dp')
The draws below stay inside these ranges and needn't reach their ends.
Inputs may be any that keep to these rules, and one draw needn't show every extreme that they name: `unit_perm`: each row is a permutation of the 5632 units. In every row, for every slab s and share g, the 352 positions s * 1408 + g * 352 up to s * 1408 + (g + 1) * 352 - 1 hold exactly 88 units of each block of 1408 consecutive units. `slab_owner`: each slab number c * 4 + s is owned by exactly one expert. `routes`: each row names 4 different experts. In each aligned block of 128 rows no expert is named more than 80 times, a bound that some block reaches.
All inputs are finite; a program needn't handle non-finite values.
Results may differ from the reference program's by a relative error of at most 0.013.
Values may be sent and summed in bfloat16 or wider, within the bound.
A program may use at most 128 MiB of HBM per device.

```python
import math
import jax
import jax.numpy as jnp
import numpy as np
from jax import lax

D = 2048
FF = 5632
EH = 1408
TOPK = 4
TOK_DEV = 128
EXPERTS = 8
SLABS = 4
COPIES = 2
UNITS_DEV = 352
PICK = 88
CAP = 80
TOKENS = 1024
N_DP = 4
N_EXPERT = 8


def draw_unit_perm(key, part):
    block_units = FF // N_DP
    key_list = jax.random.split(key, COPIES * N_DP)
    local_order = jax.vmap(lambda subkey: jax.random.permutation(subkey, block_units))(key_list)
    local_order = local_order.reshape(COPIES, N_DP, SLABS * N_DP, PICK).astype(jnp.int32)
    offsets = (jnp.arange(N_DP, dtype=jnp.int32) * block_units)[None, :, None, None]
    unit_ids = local_order + offsets
    unit_ids = jnp.transpose(unit_ids, (0, 2, 1, 3)).reshape(COPIES, SLABS * N_DP, UNITS_DEV)
    second_keys = jax.random.split(jax.random.fold_in(key, 7), COPIES * SLABS * N_DP)
    pair_order = jax.vmap(lambda subkey: jax.random.permutation(subkey, UNITS_DEV))(second_keys)
    pair_order = pair_order.reshape(COPIES, SLABS * N_DP, UNITS_DEV).astype(jnp.int32)
    unit_ids = jnp.take_along_axis(unit_ids, pair_order, axis=2)
    return unit_ids.reshape(COPIES, FF).astype(jnp.int32)


def block_scale(stream_key, shape, cuts, least, largest):
    def one(axis_at, parts):
        draws = jax.random.uniform(jax.random.fold_in(jax.random.fold_in(stream_key, 6), axis_at), (parts,), jnp.float32, least / len(cuts), largest / len(cuts))
        return jnp.repeat(jnp.exp(draws), shape[axis_at] // parts).reshape((-1,) + (1,) * (len(shape) - axis_at - 1))

    level = one(*cuts[0])
    for cut in cuts[1:]:
        level = level * one(*cut)
    return level


def assign_block(rng, own, number, rows, amount, top, bound, slope):
    order = jax.random.permutation(rng, amount)
    crowded, usual = shares(amount, rows * top, bound, slope, True), shares(amount, rows * top, bound, slope, False)
    places = jnp.arange(amount)

    def named(lengths, offset_by):
        used = int((lengths > 0).sum())
        fixed = max(1, used // 4)
        shifted = fixed + (places - fixed + offset_by * (used - fixed)) % max(1, amount - fixed)
        return jnp.zeros((amount,), jnp.int32).at[order[jnp.where(places < fixed, places, shifted)]].set(jnp.asarray(lengths, jnp.int32))

    lengths = jnp.where(number % 4 == 0, named(crowded, number // 4), named(usual, number - number // 4 - 1))
    mixed = jax.random.permutation(jax.random.fold_in(own, 3), amount)
    giver, sink = mixed[0:amount // 2 * 2:2], mixed[1:amount // 2 * 2:2]
    slack = jnp.minimum(lengths[giver] - 1, bound - lengths[sink]) // 2
    slack = jnp.where((giver == order[0]) | (sink == order[0]) | (lengths[sink] == 0), 0, jnp.maximum(slack, 0))
    shifted = jax.random.randint(jax.random.fold_in(own, 4), (amount // 2,), 0, 1 << 20) % (slack + 1)
    lengths = lengths.at[giver].add(-shifted).at[sink].add(shifted)
    labels = jnp.searchsorted(jnp.cumsum(lengths), jnp.arange(rows * top), side="right").astype(jnp.int32)
    table = labels.reshape(top, rows).T
    table = table[jax.random.permutation(jax.random.fold_in(own, 1), rows)]
    offset_by = jax.random.randint(jax.random.fold_in(own, 2), (rows, 1), 0, top)
    return jnp.take_along_axis(table, (jnp.arange(top)[None, :] + offset_by) % top, axis=1)


def shares(number_of, total, bound, slope, full):
    loads = [(1 << 20) // math.isqrt(grade ** slope) + 1 for grade in range(1, number_of + 1)]
    largest = bound if full else min(bound, max(-(-total // number_of), total * loads[0] // sum(loads)))
    least = 1 if total - largest >= number_of - 1 else 0
    given, spare = [largest] + [least] * (number_of - 1), total - largest - least * (number_of - 1)
    while spare > 0:
        movable = [i for i in range(1, number_of) if given[i] < largest] or [i for i in range(1, number_of) if given[i] < bound]
        pool, left = sum([loads[i] for i in movable]), spare
        for i in movable:
            addition = min(bound - given[i], max(1, left * loads[i] // pool), spare)
            given[i] = given[i] + addition
            spare = spare - addition
    return np.array(given)


def gaussian(rng, extent, scale, most, pieces=(), kind=jnp.bfloat16):
    loudness = block_scale(rng, extent, pieces, -0.22, 0.18) if pieces else 1.0
    values = jax.random.normal(rng, extent, jnp.float32) * scale * loudness
    return jnp.minimum(jnp.maximum(values, -most), most).astype(kind)


def setup_inputs(seed: int = 0) -> dict:
    streams_of = jax.random.split(jax.random.key(seed), 8)
    dense_weights = gaussian(streams_of[0], (3, FF, D), D ** -0.5, 0.125, ((1, 4), (2, 8)))
    tokens = gaussian(streams_of[1], (TOKENS, D), 1.0, 6.0, ((0, 8),))
    cotangent = gaussian(streams_of[2], (TOKENS, D), 1.0, 6.0, ((0, 8),))
    routes_keys = jax.random.split(jax.random.fold_in(streams_of[3], 1), TOKENS // TOK_DEV)
    routes_turns = jax.random.permutation(jax.random.fold_in(streams_of[3], 3), TOKENS // TOK_DEV)
    routes = jax.vmap(lambda own, number: assign_block(jax.random.fold_in(streams_of[3], 2), own, number, TOK_DEV, EXPERTS, TOPK, CAP, 1))(routes_keys, routes_turns).reshape((TOKENS, TOPK))
    route_gates = jnp.clip(0.2 + 0.8 * jax.random.uniform(streams_of[4], (TOKENS, TOPK), jnp.float32) ** block_scale(streams_of[4], (TOKENS, TOPK), ((0, 8),), -0.2, 0.2), 0.2, 1.0)
    unit_perm = draw_unit_perm(jax.random.fold_in(streams_of[7], 71), 0)
    slab_owner = jax.random.permutation(streams_of[6], EXPERTS).astype(jnp.int32)
    return dict(dense_weights=dense_weights, tokens=tokens, cotangent=cotangent, routes=routes, route_gates=route_gates, unit_perm=unit_perm, slab_owner=slab_owner)


def silu_parts(preact):
    sigmoid_value = jax.nn.sigmoid(preact)
    return preact * sigmoid_value, sigmoid_value * (1.0 + preact * (1.0 - sigmoid_value))


def share_products(left_side, weights):
    left_f = left_side.astype(jnp.float32).reshape(left_side.shape[0], N_DP, UNITS_DEV)
    right_f = weights.astype(jnp.float32).reshape(N_DP, UNITS_DEV, D)
    return jnp.einsum("sgu,gud->sgd", left_f, right_f)


def round_sum(share_parts):
    rounded = lax.optimization_barrier(share_parts.astype(jnp.bfloat16))
    return jnp.sum(rounded.astype(jnp.float32), axis=1)


def reference(dense_weights, tokens, cotangent, routes, route_gates, unit_perm, slab_owner):
    shared_gate = jnp.dot(tokens, dense_weights[0].T, preferred_element_type=jnp.float32)
    shared_up = jnp.dot(tokens, dense_weights[1].T, preferred_element_type=jnp.float32)
    shared_act, shared_slope = silu_parts(shared_gate)
    shared_hidden = (shared_act * shared_up).astype(jnp.bfloat16)
    shared_out = jnp.dot(shared_hidden, dense_weights[2], preferred_element_type=jnp.float32)
    shared_dh = jnp.dot(cotangent, dense_weights[2].T, preferred_element_type=jnp.float32)
    shared_dgate = (shared_dh * shared_up * shared_slope).astype(jnp.bfloat16)
    shared_dup = (shared_dh * shared_act).astype(jnp.bfloat16)
    shared_back = jnp.dot(shared_dgate, dense_weights[0], preferred_element_type=jnp.float32) + jnp.dot(shared_dup, dense_weights[1], preferred_element_type=jnp.float32)

    copies = TOKENS * TOPK
    flat_routes = routes.reshape(-1).astype(jnp.int32)
    onehot = (flat_routes[:, None] == jnp.arange(EXPERTS, dtype=jnp.int32)[None, :]).astype(jnp.int32)
    running = jnp.cumsum(onehot.reshape(N_EXPERT, TOK_DEV * TOPK, EXPERTS), axis=1).reshape(copies, EXPERTS)
    slot_rank = jnp.sum((running - 1) * onehot, axis=1)
    block_of = jnp.arange(copies, dtype=jnp.int32) // (TOK_DEV * TOPK)
    slot_index = (block_of * CAP + slot_rank).astype(jnp.int32)
    slot_table = jnp.full((EXPERTS, N_EXPERT * CAP), copies, jnp.int32).at[flat_routes, slot_index].set(jnp.arange(copies, dtype=jnp.int32))
    flat_gates = route_gates.reshape(-1)

    def expert_step(packed):
        expert, slot_rows = packed
        owned_slab = slab_owner[expert]
        copy_id = (owned_slab // SLABS).astype(jnp.int32)
        slab_start = ((owned_slab % SLABS) * EH).astype(jnp.int32)
        unit_ids = lax.dynamic_slice(unit_perm, (copy_id, slab_start), (1, EH))[0]
        weights = jnp.take(dense_weights, unit_ids, axis=1)
        filled = slot_rows < copies
        safe_rows = jnp.minimum(slot_rows, copies - 1)
        token_of = safe_rows // TOPK
        copy_x = jnp.where(filled[:, None], tokens[token_of], jnp.zeros((), jnp.bfloat16))
        gate_of = jnp.where(filled, flat_gates[safe_rows], jnp.zeros((), jnp.float32))
        copy_dy = (gate_of[:, None] * cotangent[token_of].astype(jnp.float32)).astype(jnp.bfloat16)
        pre_gate = jnp.dot(copy_x, weights[0].T, preferred_element_type=jnp.float32)
        pre_up = jnp.dot(copy_x, weights[1].T, preferred_element_type=jnp.float32)
        activation, silu_slope = silu_parts(pre_gate)
        hidden = (activation * pre_up).astype(jnp.bfloat16)
        out_rows = round_sum(share_products(hidden, weights[2]))
        d_hidden = jnp.dot(copy_dy, weights[2].T, preferred_element_type=jnp.float32)
        d_gate = (d_hidden * pre_up * silu_slope).astype(jnp.bfloat16)
        d_up = (d_hidden * activation).astype(jnp.bfloat16)
        back_rows = round_sum(share_products(d_gate, weights[0]) + share_products(d_up, weights[1]))
        weight_grads = jnp.stack([
            jnp.dot(d_gate.T, copy_x, preferred_element_type=jnp.float32),
            jnp.dot(d_up.T, copy_x, preferred_element_type=jnp.float32),
            jnp.dot(hidden.T, copy_dy, preferred_element_type=jnp.float32),
        ]).astype(jnp.bfloat16)
        return out_rows, back_rows, weight_grads

    out_rows, back_rows, expert_grad = lax.map(expert_step, (jnp.arange(EXPERTS, dtype=jnp.int32), slot_table))
    routed_out = out_rows[flat_routes, slot_index].reshape(TOKENS, TOPK, D)
    routed_back = back_rows[flat_routes, slot_index].reshape(TOKENS, TOPK, D)
    mixed = (shared_out + jnp.sum(route_gates[:, :, None] * routed_out, axis=1)).astype(jnp.bfloat16)
    token_grad = (shared_back + jnp.sum(routed_back, axis=1)).astype(jnp.bfloat16)
    return mixed, token_grad, expert_grad
```

```python
import functools

import jax
import jax.numpy as jnp
from jax import lax
from jax.experimental import pallas as pl
from jax.experimental.pallas import tpu as pltpu
from jax.sharding import PartitionSpec as P

F32 = jnp.float32
BF16 = jnp.bfloat16


def silu_parts(preact):
    sigmoid_value = jax.nn.sigmoid(preact)
    return (preact * sigmoid_value, sigmoid_value * (1.0 + preact * (1.0 - sigmoid_value)))


def dot(left, right, left_dim, right_dim):
    return lax.dot_general(
        left, right, (((left_dim,), (right_dim,)), ((), ())), preferred_element_type=F32
    )


def block_ranks(blocks, block):
    width = blocks.shape[-1]
    mask = blocks == block
    upper = lax.broadcasted_iota(jnp.int32, (width, width), 0) < lax.broadcasted_iota(
        jnp.int32, (width, width), 1
    )
    rank = jnp.dot(mask.astype(BF16), upper.astype(BF16), preferred_element_type=F32)
    return mask, rank.astype(jnp.int32)


def log2(count):
    return count.bit_length() - 1


def flip(index, place):
    return index + (1 - 2 * (index // (1 << place) % 2)) * (1 << place)


def peer(device, n_ex):
    return {"dp": device // n_ex, "expert": device % n_ex}


STREAMS = 4


def halving_orders(dp_bits, ex_bits):
    rest = [ex_bits + bit for bit in range(1, dp_bits)] + list(range(ex_bits))
    turns = [[0, 1, 2], [1, 2, 0], [2, 0, 1], [1, 0, 2]]
    orders = []
    for turn in turns:
        head = [rest[at] for at in turn if at < len(rest)]
        orders.append([ex_bits] + head + rest[len(head) :])
    return orders


def halving_kernel(n_dp, n_ex, n_arrays, with_grads, *refs):
    ins, refs = refs[:n_arrays], refs[n_arrays:]
    acts, order_ref, fulls, refs = (
        (refs[:3], refs[3], refs[4:6], refs[6:]) if with_grads else ((), None, (), refs)
    )
    outs, refs = refs[:n_arrays], refs[n_arrays:]
    if with_grads:
        grads, full_rows, grad_rows, act_rows, full_sem, grad_sem = refs[0], *refs[-5:]
        refs = refs[1:-5]
    data, recv, load_sem, send_sem, recv_sem = refs
    me = lax.axis_index("dp") * n_ex + lax.axis_index("expert")
    bits = log2(n_dp) + log2(n_ex)
    orders = halving_orders(log2(n_dp), log2(n_ex))
    rows, part = data.shape[2:]
    splits = STREAMS // n_arrays

    for stream in range(STREAMS):
        source, at = ins[stream // splits], stream % splits
        for g in range(n_dp):

            def load(e, carry, source=source, at=at, g=g, stream=stream):
                start = pl.multiple_of(e * (rows * splits) + at * rows, rows)
                pltpu.make_async_copy(
                    source.at[pl.ds(start, rows), pl.ds(g * part, part)],
                    data.at[stream, g * n_ex + e],
                    load_sem.at[stream],
                ).start()
                return carry

            lax.fori_loop(0, n_ex, load, 0)

    for at, full in enumerate(fulls):
        pltpu.make_async_copy(full, full_rows.at[at], full_sem.at[at]).start()

    def weight_grad(k):
        if k != 1:
            at = k // 2
            pltpu.make_async_copy(fulls[at], full_rows.at[at], full_sem.at[at]).wait()
        width = full_rows.shape[-1]
        piece = min(512, width)
        act_rows[...] = dot(order_ref[...], acts[k][...], 1, 1).astype(BF16)

        def product(step, carry):
            lanes = pl.ds(pl.multiple_of(step * piece, piece), piece)
            grad_rows[k, :, lanes] = jnp.dot(
                act_rows[...], full_rows[k // 2, :, lanes], preferred_element_type=F32
            ).astype(BF16)
            return carry

        lax.fori_loop(0, width // piece, product, 0)
        pltpu.make_async_copy(grad_rows.at[k], grads.at[0, k], grad_sem.at[k]).start()

    barrier = pltpu.get_barrier_semaphore()
    for place in range(bits):
        pl.semaphore_signal(
            barrier,
            inc=1,
            device_id=peer(flip(me, place), n_ex),
            device_id_type=pl.DeviceIdType.MESH,
        )
    pl.semaphore_wait(barrier, bits)

    def block_of(stream, step, choice, sent):
        order = orders[stream]
        index = 0
        for place in order[: step + 1]:
            index = index + me // (1 << place) % 2 * (1 << place)
        if sent:
            index = flip(index, order[step])
        for bit, place in enumerate(sorted(order[step + 1 :])):
            index = index + choice // (1 << bit) % 2 * (1 << place)
        return index

    def count(step):
        return 1 << (bits - 1 - step)

    def offset(step):
        return (1 << bits) - (1 << (bits - step))

    def send(stream, step, choice):
        pltpu.make_async_remote_copy(
            src_ref=data.at[stream, block_of(stream, step, choice, True)],
            dst_ref=recv.at[stream, offset(step) + choice],
            send_sem=send_sem.at[stream, step],
            recv_sem=recv_sem.at[stream, step],
            device_id=peer(flip(me, orders[stream][step]), n_ex),
            device_id_type=pl.DeviceIdType.MESH,
        ).start()

    def region(stream, step):
        view = recv.at[stream, pl.ds(offset(step), count(step))]
        return pltpu.make_async_remote_copy(
            src_ref=view,
            dst_ref=view,
            send_sem=send_sem.at[stream, step],
            recv_sem=recv_sem.at[stream, step],
            device_id=peer(flip(me, orders[stream][step]), n_ex),
            device_id_type=pl.DeviceIdType.MESH,
        )

    def number(stream, step, choice, sent):
        order = orders[stream]
        later = sorted(order[step + 1 :])
        place = order[step + 1]
        mine = me // (1 << place) % 2
        value = (1 - mine if sent else mine) * (1 << later.index(place))
        for bit, other in enumerate(sorted(order[step + 2 :])):
            value = value + choice // (1 << bit) % 2 * (1 << later.index(other))
        return value

    for stream in range(STREAMS):
        pltpu.make_async_copy(data.at[stream], data.at[stream], load_sem.at[stream]).wait()

        def first(choice, carry, stream=stream):
            send(stream, 0, choice)
            return carry

        lax.fori_loop(0, count(0), first, 0)

    if with_grads:
        weight_grad(0)
    for step in range(bits):
        for stream in range(STREAMS):
            region(stream, step).wait_recv()
            if step == bits - 1:
                total = data[stream, me].astype(F32) + recv[stream, offset(step)].astype(F32)
                outs[stream // splits][pl.ds(stream % splits * rows, rows), :] = total.astype(BF16)
                continue
            for sent in (True, False):

                def add(choice, carry, stream=stream, step=step, sent=sent):
                    block = block_of(stream, step + 1, choice, sent)
                    slot = offset(step) + number(stream, step, choice, sent)
                    total = data[stream, block].astype(F32) + recv[stream, slot].astype(F32)
                    data[stream, block] = total.astype(BF16)
                    if sent:
                        send(stream, step + 1, choice)
                    return carry

                lax.fori_loop(0, count(step + 1), add, 0)
        if step < 2 and with_grads:
            weight_grad(step + 1)

    if with_grads:
        for k in range(3):
            pltpu.make_async_copy(grad_rows.at[k], grads.at[0, k], grad_sem.at[k]).wait()
    for step in range(bits):
        for stream in range(STREAMS):
            region(stream, step).wait_send()


def halving_sum(n_dp, n_ex, arrays, acts=(), fulls=()):
    total, width = arrays[0].shape
    tok, part, n_arrays = total // n_ex, width // n_dp, len(arrays)
    rows = tok * n_arrays // STREAMS
    blocks = n_dp * n_ex
    steps = log2(blocks)
    any_spec, vmem_spec = pl.BlockSpec(memory_space=pl.ANY), pl.BlockSpec(memory_space=pltpu.VMEM)
    out_shape = [jax.ShapeDtypeStruct((tok, part), BF16)] * n_arrays
    out_specs = [vmem_spec] * n_arrays
    scratch = [
        pltpu.VMEM((STREAMS, blocks, rows, part), BF16),
        pltpu.VMEM((STREAMS, blocks - 1, rows, part), BF16),
        pltpu.SemaphoreType.DMA((STREAMS,)),
        pltpu.SemaphoreType.DMA((STREAMS, steps)),
        pltpu.SemaphoreType.DMA((STREAMS, steps)),
    ]
    if acts:
        share = acts[0].shape[1]
        out_shape = out_shape + [jax.ShapeDtypeStruct((1, 3, share, width), BF16)]
        out_specs = out_specs + [any_spec]
        scratch = scratch + [
            pltpu.VMEM((2, total, width), BF16),
            pltpu.VMEM((3, share, width), BF16),
            pltpu.VMEM((share, total), BF16),
            pltpu.SemaphoreType.DMA((2,)),
            pltpu.SemaphoreType.DMA((3,)),
        ]
    return pl.pallas_call(
        functools.partial(halving_kernel, n_dp, n_ex, n_arrays, bool(acts)),
        out_shape=out_shape,
        in_specs=[any_spec] * n_arrays + [vmem_spec] * len(acts) + [any_spec] * len(fulls),
        out_specs=out_specs,
        scratch_shapes=scratch,
        compiler_params=pltpu.CompilerParams(
            collective_id=1, has_side_effects=True, vmem_limit_bytes=60 << 20
        ),
        name="halving_sum",
    )(*arrays, *acts, *fulls)


def flip_mask(index, mask):
    place = 0
    while mask >> place:
        if mask >> place & 1:
            index = flip(index, place)
        place += 1
    return index


def fused_kernel(n_dp, n_ex, *refs):
    shares, owner, table, dense, tokens, cotangent, mixed, token_grad, grads, *refs = refs
    side, full, picked, weights, pre, mult, own_acts, far_acts, *refs = refs
    data, recv, swap, upper, order_ref, act_rows, grad_rows, gates, gate_col, both_col, *refs = refs
    load_sem, gate_sem, row_send, row_recv, fwd_send, fwd_recv, tok_send, tok_recv, *refs = refs
    act_sem, halve_send, halve_recv, swap_sem, out_sem = refs

    row, col = lax.axis_index("dp"), lax.axis_index("expert")
    me = row * n_ex + col
    core, spot_x = row % 2, row // 2
    n_x = n_dp // 2
    chip = spot_x * n_ex + col
    block_units, feat = side.shape[1:]
    pick, share = picked.shape[2], shares.shape[2]
    padded = weights.shape[1] // (2 * n_dp)
    half_units = n_dp * padded
    width = full.shape[2]
    tok = tokens.shape[0]
    quarter = tok // n_dp
    half = full.shape[1] // 2
    dp_bits, ex_bits = log2(n_dp), log2(n_ex)
    bits = dp_bits + ex_bits
    sibling = peer(flip(me, ex_bits), n_ex)
    mesh_id = pl.DeviceIdType.MESH

    def remote(src, dst, send_sem, recv_sem, device):
        return pltpu.make_async_remote_copy(
            src_ref=src,
            dst_ref=dst,
            send_sem=send_sem,
            recv_sem=recv_sem,
            device_id=device,
            device_id_type=mesh_id,
        )

    def wait(view, sem):
        pltpu.make_async_copy(view, view, sem).wait()

    def place(at, device):
        where = device // n_ex
        start = where % 2 * half + where // 2 * (n_ex * quarter) + device % n_ex * quarter
        return full.at[at, pl.ds(pl.multiple_of(start, quarter), quarter), :]

    for at, source in enumerate((tokens, cotangent)):
        pltpu.make_async_copy(
            source.at[pl.ds(pl.multiple_of(row * quarter, quarter), quarter), :],
            place(at, me),
            load_sem.at[at],
        ).start()
    pltpu.make_async_copy(dense, side, load_sem.at[2]).start()
    pltpu.make_async_copy(table.at[col], gates.at[col], gate_sem.at[1]).start()

    if padded > pick:
        for k in range(3):
            for slot in range(2 * n_dp):
                rows = pl.ds(slot * padded + pick, padded - pick)
                weights[k, rows, :] = jnp.zeros((padded - pick, width), BF16)

    barrier = pltpu.get_barrier_semaphore()
    for mask in range(1, n_dp * n_ex):
        pl.semaphore_signal(
            barrier, inc=1, device_id=peer(flip_mask(me, mask), n_ex), device_id_type=mesh_id
        )
    upper[...] = (
        lax.broadcasted_iota(jnp.int32, (share, share), 0)
        < lax.broadcasted_iota(jnp.int32, (share, share), 1)
    ).astype(BF16)
    pl.semaphore_wait(barrier, n_dp * n_ex - 1)

    for at in range(2):
        wait(place(at, me), load_sem.at[at])

    ex_order = list(range(ex_bits - 1, -1, -1))
    dp_order = [ex_bits + bit for bit in range(dp_bits - 1, -1, -1)]
    tok_orders = [
        ex_order + dp_order,
        ex_order[:-1] + [dp_order[0], ex_order[-1]] + dp_order[1:],
    ]

    def send_tokens(step):
        for at in range(2):
            order = tok_orders[at]

            def one(choice, carry, at=at, order=order):
                device = me
                for bit, other in enumerate(order[:step]):
                    mine = me // (1 << other) % 2
                    device = device + (choice // (1 << bit) % 2 - mine) * (1 << other)
                remote(
                    place(at, device),
                    place(at, device),
                    tok_send.at[at, step],
                    tok_recv.at[at, step],
                    peer(flip(me, order[step]), n_ex),
                ).start()
                return carry

            lax.fori_loop(0, 1 << step, one, 0)

    def wait_tokens(step, sem):
        for at in range(2):
            wait(full.at[at, pl.ds(0, (1 << step) * quarter), :], sem.at[at, step])

    send_tokens(0)
    for mask in range(1, n_ex):
        device = flip_mask(me, mask)
        remote(
            table.at[device % n_ex],
            gates.at[col],
            gate_sem.at[0],
            gate_sem.at[1],
            peer(device, n_ex),
        ).start()
    wait(side, load_sem.at[2])

    def ranks(mask):
        return jnp.dot(mask.astype(BF16), upper[...], preferred_element_type=F32)

    def send_rows(mask):
        target = flip_mask(col, mask)
        local = shares[owner[target]] - row * block_units
        inside = jnp.logical_and(local >= 0, local < block_units)
        spots = jnp.where(inside, ranks(inside), -1.0)
        values = (local + 1).astype(F32)
        hots = []
        for g in range(n_dp):
            hit = spots[g : g + 1, :] == lax.broadcasted_iota(
                jnp.int32, (padded, share), 0
            ).astype(F32)
            units = jnp.sum(jnp.where(hit, values[g : g + 1, :], 0.0), axis=1, keepdims=True)
            hots.append(
                (
                    units.astype(jnp.int32) - 1
                    == lax.broadcasted_iota(jnp.int32, (padded, block_units), 1)
                ).astype(BF16)
            )
        hot = jnp.concatenate(hots, axis=0)
        for k in range(3):
            rows = jnp.dot(hot, side[k], preferred_element_type=F32).astype(BF16)
            for g in range(n_dp):
                picked[mask * n_dp + g, k] = rows[g * padded : g * padded + pick, :]
        for turn in range(n_dp):
            g = flip_mask(row, turn)

            def one(k, carry, g=g, turn=turn):
                source = picked.at[mask * n_dp + g, k]
                start = pl.multiple_of((g % 2 * n_dp + row) * padded, padded)
                target_ref = weights.at[
                    k,
                    pl.ds(start, pick),
                    pl.ds(pl.multiple_of(col * feat, feat), feat),
                ]
                if mask == 0 and turn == 0:
                    pltpu.make_async_copy(source, target_ref, row_recv.at[col]).start()
                else:
                    remote(
                        source,
                        target_ref,
                        row_send.at[0],
                        row_recv.at[col],
                        {"dp": g, "expert": target},
                    ).start()
                return carry

            lax.fori_loop(0, 3, one, 0)

    far, near = [m for m in range(n_ex) if m >= n_ex // 2], [m for m in range(1, n_ex // 2)] + [0]
    masks = [m for pair in zip(far, near) for m in pair]
    per_step = 2
    for step in range(bits - 1):
        for mask in masks[step * per_step : (step + 1) * per_step]:
            send_rows(mask)
        wait_tokens(step, tok_recv)
        send_tokens(step + 1)
    for mask in masks[(bits - 1) * per_step :]:
        send_rows(mask)

    mine = shares[owner[col], pl.ds(row, 1), :]
    at_row = jnp.zeros((1, share), F32)
    for b in range(n_dp):
        inside = jnp.logical_and(mine >= b * block_units, mine < (b + 1) * block_units)
        at_row = at_row + jnp.where(inside, ranks(inside) + float(b * padded), 0.0)
    diagonal = lax.broadcasted_iota(jnp.int32, (share, share), 0) == lax.broadcasted_iota(
        jnp.int32, (share, share), 1
    )
    at_col = jnp.sum(jnp.where(diagonal, at_row, 0.0), axis=1, keepdims=True)
    order_ref[...] = (
        at_col.astype(jnp.int32) == lax.broadcasted_iota(jnp.int32, (share, half_units), 1)
    ).astype(BF16)

    wait(table.at[pl.ds(0, n_ex - 1)], gate_sem.at[0])
    wait(gates, gate_sem.at[1])
    copy_id = owner[col] // (n_ex // 2)
    lanes = lax.broadcasted_iota(jnp.int32, (quarter, tok), 1)
    below = lax.broadcasted_iota(jnp.int32, (quarter, tok), 0)
    for xq in range(n_x):

        def column(block, carry, xq=xq):
            hit = lanes == below + (xq * 2 + core) * quarter
            value = jnp.sum(jnp.where(hit, gates[block], 0.0), axis=1, keepdims=True)
            value = jnp.broadcast_to(value, (quarter, 128))
            blocks = jnp.full((quarter, 128), block * 2 // n_ex, jnp.int32)
            rows = pl.ds(pl.multiple_of((xq * n_ex + block) * quarter, quarter), quarter)
            gate_col[rows, :] = value
            both_col[rows, :] = value + (blocks == copy_id).astype(F32)
            return carry

        lax.fori_loop(0, n_ex, column, 0)

    my_rows = pl.ds(pl.multiple_of(core * half, half), half)
    my_units = pl.ds(pl.multiple_of(core * half_units, half_units), half_units)
    far_units = pl.ds(pl.multiple_of((1 - core) * half_units, half_units), half_units)
    n_tile = min(256, 2 * half_units)
    tiles = 2 * half_units // n_tile

    def columns(mask):
        return pl.ds(pl.multiple_of(flip_mask(col, mask) * feat, feat), feat)

    def forward(mask):
        f = flip_mask(col, mask)
        count = n_dp * pick
        wait(weights.at[:, pl.ds(0, count), columns(mask)], row_recv.at[f])
        for k in range(3):
            view = weights.at[k, my_units, columns(mask)]
            remote(view, view, fwd_send.at[0], fwd_recv.at[f], sibling).start()

    def accumulate(mask, first):
        f = flip_mask(col, mask)
        wait(weights.at[:, far_units, columns(mask)], fwd_recv.at[f])

        def one(index, carry):
            k, n = index // tiles, index % tiles
            units = pl.ds(pl.multiple_of(n * n_tile, n_tile), n_tile)
            value = dot(full[k // 2, my_rows, columns(mask)], weights[k, units, columns(mask)], 1, 1)
            if first:
                pre[k, :, units] = value
            else:
                pre[k, :, units] = pre[k, :, units] + value
            return carry

        lax.fori_loop(0, 3 * tiles, one, 0)

    for at, mask in enumerate(masks):
        forward(mask)
        if at:
            accumulate(masks[at - 1], at == 1)
    accumulate(masks[-1], False)

    r_tile = 32

    def activate(share_at, keep):
        units = pl.ds(pl.multiple_of(share_at * half_units, half_units), half_units)

        def one(index, carry):
            rows = pl.ds(pl.multiple_of(index * r_tile, r_tile), r_tile)
            reps = (1, half_units // 128)
            gate = jnp.tile(gate_col[rows, :], reps)
            both = jnp.tile(both_col[rows, :], reps)
            act, slope = silu_parts(pre[0, rows, units])
            up, d_hidden = pre[1, rows, units], pre[2, rows, units]
            values = (d_hidden * up * slope, d_hidden * act, act * up)
            for k, value in enumerate(values):
                mult[k, rows, units] = (both * value).astype(BF16)
                if keep:
                    own_acts[core, k, rows, :] = (gate * value).astype(BF16)
                else:
                    far_acts[k, rows, :] = (gate * value).astype(BF16)
            return carry

        lax.fori_loop(0, half // r_tile, one, 0)

    activate(1 - core, False)
    act_copy = remote(far_acts, own_acts.at[core], act_sem.at[0], act_sem.at[1], sibling)
    act_copy.start()
    activate(core, True)

    chip_bits = bits - 1
    x_place, y_place, z_low = chip_bits - 1, 0, 1
    rest = list(range(2, chip_bits - 1))
    classes = {
        "a": [x_place, y_place, z_low] + rest,
        "b": [y_place, z_low, x_place] + rest,
        "c": [z_low, x_place, y_place] + rest,
    }
    kinds = ["a", "a", "a", "c", "b", "b", "b", "c"]
    turns = [0, 4, 3, 1, 5, 7, 2, 6]
    chunk = data.shape[3]
    per_array = width // n_x // chunk
    r_rows = data.shape[2]

    def chip_peer(place_at):
        if place_at == x_place:
            return peer(flip(me, bits - 1), n_ex)
        return peer(flip(me, place_at), n_ex)

    def block_of(stream, step, choice, sent):
        order = classes[kinds[stream]]
        index = 0
        for place_at in order[: step + 1]:
            index = index + chip // (1 << place_at) % 2 * (1 << place_at)
        if sent:
            index = flip(index, order[step])
        for bit, place_at in enumerate(sorted(order[step + 1 :])):
            index = index + choice // (1 << bit) % 2 * (1 << place_at)
        return index

    def count(step):
        return 1 << (chip_bits - 1 - step)

    def offset(step):
        return (1 << chip_bits) - (1 << (chip_bits - step))

    def send(stream, step, choice):
        remote(
            data.at[stream, block_of(stream, step, choice, True)],
            recv.at[stream, offset(step) + choice],
            halve_send.at[stream, step],
            halve_recv.at[stream, step],
            chip_peer(classes[kinds[stream]][step]),
        ).start()

    def region(stream, step):
        return recv.at[stream, pl.ds(offset(step), count(step))]

    def number(stream, step, choice, sent):
        order = classes[kinds[stream]]
        later = sorted(order[step + 1 :])
        place_at = order[step + 1]
        mine_bit = chip // (1 << place_at) % 2
        value = (1 - mine_bit if sent else mine_bit) * (1 << later.index(place_at))
        for bit, other in enumerate(sorted(order[step + 2 :])):
            value = value + choice // (1 << bit) % 2 * (1 << later.index(other))
        return value

    def product(stream, xq):
        array, j = stream // per_array, stream % per_array
        cols = pl.ds(pl.multiple_of(xq * (width // n_x) + j * chunk, chunk), chunk)
        if array == 0:
            value = jnp.dot(mult[2], weights[2, :, cols], preferred_element_type=F32)
        else:
            value = jnp.dot(mult[0], weights[0, :, cols], preferred_element_type=F32)
            value = value + jnp.dot(mult[1], weights[1, :, cols], preferred_element_type=F32)
        value = value.astype(BF16).reshape(n_x, n_ex, quarter, chunk)
        for part in range(n_x):
            data[
                stream,
                pl.ds(pl.multiple_of(xq * n_ex, n_ex), n_ex),
                part * quarter : (part + 1) * quarter,
                :,
            ] = value[part]

    def begin(stream):
        def first(choice, carry):
            send(stream, 0, choice)
            return carry

        lax.fori_loop(0, count(0), first, 0)

    for stream in turns:
        if kinds[stream] == "a":
            product(stream, 1 - spot_x)
            begin(stream)
        else:

            def both_sides(side_at, carry, stream=stream):
                product(stream, side_at)
                return carry

            lax.fori_loop(0, n_x, both_sides, 0)
            begin(stream)
    for stream in turns:
        if kinds[stream] == "a":
            product(stream, spot_x)

    def weight_grad(k):
        for part in range(2):
            act_rows[:, part * half : (part + 1) * half] = dot(
                order_ref[...], own_acts[part, k], 1, 1
            ).astype(BF16)
        piece = min(512, width)

        def one(step, carry):
            where = pl.ds(pl.multiple_of(step * piece, piece), piece)
            grad_rows[k, :, where] = jnp.dot(
                act_rows[...], full[k // 2, :, where], preferred_element_type=F32
            ).astype(BF16)
            return carry

        lax.fori_loop(0, width // piece, one, 0)
        pltpu.make_async_copy(grad_rows.at[k], grads.at[0, k], out_sem.at[k]).start()

    def combine(stream, step):
        wait(region(stream, step), halve_recv.at[stream, step])
        for sent in (True, False):

            def add(choice, carry, sent=sent):
                block = block_of(stream, step + 1, choice, sent)
                slot = offset(step) + number(stream, step, choice, sent)
                total = data[stream, block].astype(F32) + recv[stream, slot].astype(F32)
                data[stream, block] = total.astype(BF16)
                if sent:
                    send(stream, step + 1, choice)
                return carry

            lax.fori_loop(0, count(step + 1), add, 0)

    wait_tokens(bits - 1, tok_recv)
    act_copy.wait()
    fill = {(0, 0): 0, (0, 3): 1, (0, 6): 2}
    for step in range(chip_bits - 1):
        for at, stream in enumerate(turns):
            if (step, at) in fill:
                weight_grad(fill[step, at])
            combine(stream, step)

    last = chip_bits - 1
    results = (mixed, token_grad)

    def finish(array, i, keep):
        owner_core = core if keep else 1 - core
        stream = array * per_array + owner_core * (per_array // 2) + i
        wait(recv.at[stream, pl.ds(offset(last), 1)], halve_recv.at[stream, last])
        total = (
            data[stream, chip].astype(F32) + recv[stream, offset(last)].astype(F32)
        ).astype(BF16)
        if keep:
            put(array, i, core, total)
        else:
            data[stream, chip] = total
            remote(
                data.at[stream, chip],
                swap.at[array, i],
                swap_sem.at[0],
                swap_sem.at[1],
                sibling,
            ).start()

    def put(array, i, which, total):
        for part in range(n_x):
            start = pl.multiple_of((part * 2 + which) * quarter, quarter)
            results[array][pl.ds(start, quarter), i * chunk : (i + 1) * chunk] = total[
                part * quarter : (part + 1) * quarter
            ]

    for keep in (False, True):
        for array in range(2):
            for i in range(per_array // 2):
                finish(array, i, keep)
    wait(swap, swap_sem.at[1])
    for array in range(2):
        for i in range(per_array // 2):
            put(array, i, 1 - core, swap[array, i])

    for k in range(3):
        pltpu.make_async_copy(grad_rows.at[k], grads.at[0, k], out_sem.at[k]).wait()
    wait(picked.at[pl.ds(0, n_dp * n_ex - 1)], row_send.at[0])
    wait(weights.at[:, my_units, :], fwd_send.at[0])
    for step in range(bits):
        wait_tokens(step, tok_send)
    for step in range(chip_bits):
        for stream in range(len(kinds)):
            wait(region(stream, step), halve_send.at[stream, step])
    wait(swap, swap_sem.at[0])


def fused_step(n_dp, n_ex, shares, slab_owner, table, dense_weights, tokens, cotangent):
    _, block_units, feat = dense_weights.shape
    tok, width = tokens.shape
    share = shares.shape[2]
    pick = share // n_dp
    padded = -(-pick // 16) * 16
    half_units, half = n_dp * padded, n_ex * tok // 2
    blocks, bits, n_x = n_dp * n_ex, log2(n_dp * n_ex), n_dp // 2
    chips, chunk = blocks // 2, 256
    streams = 2 * (width // n_x // chunk)
    any_spec, vmem_spec = pl.BlockSpec(memory_space=pl.ANY), pl.BlockSpec(memory_space=pltpu.VMEM)
    r_rows = tok // 2
    return pl.pallas_call(
        functools.partial(fused_kernel, n_dp, n_ex),
        out_shape=[
            jax.ShapeDtypeStruct((tok, width // n_dp), BF16),
            jax.ShapeDtypeStruct((tok, width // n_dp), BF16),
            jax.ShapeDtypeStruct((1, 3, share, width), BF16),
        ],
        in_specs=[
            vmem_spec,
            pl.BlockSpec(memory_space=pltpu.SMEM),
            vmem_spec,
            any_spec,
            any_spec,
            any_spec,
        ],
        out_specs=[vmem_spec, vmem_spec, any_spec],
        scratch_shapes=[
            pltpu.VMEM((3, block_units, feat), BF16),
            pltpu.VMEM((2, n_ex * tok, width), BF16),
            pltpu.VMEM((blocks, 3, pick, feat), BF16),
            pltpu.VMEM((3, 2 * half_units, width), BF16),
            pltpu.VMEM((3, half, 2 * half_units), F32),
            pltpu.VMEM((3, half, 2 * half_units), BF16),
            pltpu.VMEM((2, 3, half, half_units), BF16),
            pltpu.VMEM((3, half, half_units), BF16),
            pltpu.VMEM((streams, chips, r_rows, chunk), BF16),
            pltpu.VMEM((streams, chips - 1, r_rows, chunk), BF16),
            pltpu.VMEM((2, streams // 4, r_rows, chunk), BF16),
            pltpu.VMEM((share, share), BF16),
            pltpu.VMEM((share, half_units), BF16),
            pltpu.VMEM((share, n_ex * tok), BF16),
            pltpu.VMEM((3, share, width), BF16),
            pltpu.VMEM((n_ex, 1, tok), F32),
            pltpu.VMEM((half, 128), F32),
            pltpu.VMEM((half, 128), F32),
            pltpu.SemaphoreType.DMA((3,)),
            pltpu.SemaphoreType.DMA((2,)),
            pltpu.SemaphoreType.DMA((1,)),
            pltpu.SemaphoreType.DMA((n_ex,)),
            pltpu.SemaphoreType.DMA((1,)),
            pltpu.SemaphoreType.DMA((n_ex,)),
            pltpu.SemaphoreType.DMA((2, bits)),
            pltpu.SemaphoreType.DMA((2, bits)),
            pltpu.SemaphoreType.DMA((2,)),
            pltpu.SemaphoreType.DMA((streams, bits - 1)),
            pltpu.SemaphoreType.DMA((streams, bits - 1)),
            pltpu.SemaphoreType.DMA((2,)),
            pltpu.SemaphoreType.DMA((3,)),
        ],
        compiler_params=pltpu.CompilerParams(
            collective_id=2, has_side_effects=True, vmem_limit_bytes=63 << 20
        ),
        name="fused_step",
    )(shares, slab_owner, table.reshape(n_ex, 1, tok), dense_weights, tokens, cotangent)


def gather_plain(n_dp, n_ex, row, picked, tokens, cotangent, table):
    _, pick, wide = picked.shape
    tok, width = tokens.shape
    arrived = lax.all_to_all(picked, ("dp", "expert"), split_axis=0, concat_axis=0, tiled=True)
    arrived = arrived.reshape(n_dp, n_ex, pick, 3, wide // 3)
    weights = jnp.transpose(arrived, (3, 0, 2, 1, 4)).reshape(3, n_dp * pick, width)
    part = width // n_dp
    both = jnp.concatenate(
        [
            lax.dynamic_slice(tokens, (0, row * part), (tok, part)),
            lax.dynamic_slice(cotangent, (0, row * part), (tok, part)),
        ],
        axis=1,
    )
    both = lax.all_gather(both, "expert", axis=0, tiled=True)
    both = lax.all_gather(both, "dp", axis=0, tiled=False)
    all_x = jnp.transpose(both[:, :, :part], (1, 0, 2)).reshape(n_ex * tok, width)
    all_c = jnp.transpose(both[:, :, part:], (1, 0, 2)).reshape(n_ex * tok, width)
    gates = lax.all_to_all(table, "expert", split_axis=0, concat_axis=0, tiled=True)
    return weights, all_x, all_c, gates


def body(dense_weights, tokens, cotangent, routes, route_gates, unit_perm, slab_owner):
    n_dp = lax.axis_size("dp")
    n_ex = lax.axis_size("expert")
    row = lax.axis_index("dp")
    col = lax.axis_index("expert")
    _, block_units, feat = dense_weights.shape
    copies, total_units = unit_perm.shape
    slabs = n_ex // copies
    slab_units = total_units // slabs
    share = slab_units // n_dp
    pick = share // n_dp
    tok, width = tokens.shape

    shares = unit_perm.reshape(n_ex, n_dp, share)
    gate_table = jnp.sum(
        jnp.where(
            routes[None, :, :] == lax.broadcasted_iota(jnp.int32, (n_ex, 1, 1), 0),
            route_gates[None, :, :],
            0.0,
        ),
        axis=2,
    )
    padded = -(-pick // 16) * 16
    if (
        copies == 2
        and pick % 8 == 0
        and feat % 256 == 0
        and n_dp * padded % 128 == 0
        and 2 * n_dp * padded % 256 == 0
        and n_dp == 4
        and n_ex == 8
        and width == n_dp * 512
        and tok == 128
    ):
        return tuple(
            fused_step(
                n_dp, n_ex, shares, slab_owner, gate_table, dense_weights, tokens, cotangent
            )
        )
    dest = jnp.transpose(shares[slab_owner], (1, 0, 2)).reshape(n_dp * n_ex, share)
    mask, rank = block_ranks(dest // block_units, row)
    place = jnp.where(mask, rank, -1)
    hit = place[:, None, :] == lax.broadcasted_iota(jnp.int32, (1, pick, 1), 1)
    units = jnp.sum(jnp.where(hit, (dest - row * block_units)[:, None, :], 0), axis=2)
    onehot = (
        units.reshape(-1, 1) == lax.broadcasted_iota(jnp.int32, (1, block_units), 1)
    ).astype(BF16)
    side = jnp.concatenate([dense_weights[0], dense_weights[1], dense_weights[2]], axis=1)
    picked = dot(onehot, side, 1, 0).astype(BF16)
    picked = picked.reshape(n_dp * n_ex, pick, 3 * feat)
    mine = lax.dynamic_slice(
        shares, (slab_owner[col], row, 0), (1, 1, share)
    ).reshape(1, share)
    mine_block = mine // block_units
    mask, rank = block_ranks(
        jnp.broadcast_to(mine_block, (n_dp, share)),
        lax.broadcasted_iota(jnp.int32, (n_dp, 1), 0),
    )
    at = jnp.sum(
        jnp.where(mask, rank + lax.broadcasted_iota(jnp.int32, (n_dp, 1), 0) * pick, 0), axis=0
    )
    order = (lax.broadcasted_iota(jnp.int32, (share, share), 1) == at[:, None]).astype(BF16)

    weights, all_x, all_c, gate = gather_plain(
        n_dp, n_ex, row, picked, tokens, cotangent, gate_table
    )
    w_gate, w_up, w_down = weights[0], weights[1], weights[2]
    gate = gate.reshape(n_ex * tok, 1)
    copy_id = slab_owner[col] // slabs
    owner_block = lax.broadcasted_iota(jnp.int32, (n_ex, tok), 0).reshape(n_ex * tok, 1)
    both_weight = gate + (owner_block * copies // n_ex == copy_id).astype(F32)

    pre_gate = dot(all_x, w_gate, 1, 1)
    pre_up = dot(all_x, w_up, 1, 1)
    d_hidden = dot(all_c, w_down, 1, 1)
    act, slope = silu_parts(pre_gate)
    hidden = act * pre_up
    d_gate = d_hidden * pre_up * slope
    d_up = d_hidden * act

    out = dot((both_weight * hidden).astype(BF16), w_down, 1, 0).astype(BF16)
    back = (
        dot((both_weight * d_gate).astype(BF16), w_gate, 1, 0)
        + dot((both_weight * d_up).astype(BF16), w_up, 1, 0)
    ).astype(BF16)

    acts = [(gate * values).astype(BF16) for values in (d_gate, d_up, hidden)]
    if out.size * out.dtype.itemsize <= 1 << 23:
        mixed, token_grad, weight_grads = halving_sum(
            n_dp, n_ex, [out, back], acts + [order], [all_x, all_c]
        )
    else:
        acts = [dot(order, values, 1, 1).astype(BF16) for values in acts]
        weight_grads = jnp.stack(
            [dot(acts[0], all_x, 1, 0), dot(acts[1], all_x, 1, 0), dot(acts[2], all_c, 1, 0)]
        ).astype(BF16)[None]
        (mixed,) = halving_sum(n_dp, n_ex, [out])
        (token_grad,) = halving_sum(n_dp, n_ex, [back])
    return (mixed, token_grad, weight_grads)


def solution(mesh):
    in_specs = (
        P(None, "dp", "expert"),
        P("expert", None),
        P("expert", None),
        P("expert", None),
        P("expert", None),
        P(),
        P(),
    )
    out_specs = (P("expert", "dp"), P("expert", "dp"), P("expert", None, "dp", None))
    return jax.shard_map(body, mesh=mesh, in_specs=in_specs, out_specs=out_specs, check_vma=False)
```

```python
import functools

import jax
import jax.numpy as jnp
from jax import lax
from jax.experimental import pallas as pl
from jax.experimental.pallas import tpu as pltpu
from jax.sharding import PartitionSpec as P

F32 = jnp.float32
BF16 = jnp.bfloat16


def silu_parts(preact):
    sigmoid_value = jax.nn.sigmoid(preact)
    return (preact * sigmoid_value, sigmoid_value * (1.0 + preact * (1.0 - sigmoid_value)))


def dot(left, right, left_dim, right_dim):
    return lax.dot_general(
        left, right, (((left_dim,), (right_dim,)), ((), ())), preferred_element_type=F32
    )


def block_ranks(blocks, block):
    width = blocks.shape[-1]
    mask = blocks == block
    upper = lax.broadcasted_iota(jnp.int32, (width, width), 0) < lax.broadcasted_iota(
        jnp.int32, (width, width), 1
    )
    rank = jnp.dot(mask.astype(BF16), upper.astype(BF16), preferred_element_type=F32)
    return mask, rank.astype(jnp.int32)


def log2(count):
    return count.bit_length() - 1


def flip(index, place):
    return index + (1 - 2 * (index // (1 << place) % 2)) * (1 << place)


def peer(device, n_ex):
    return {"dp": device // n_ex, "expert": device % n_ex}


STREAMS = 4


def halving_orders(dp_bits, ex_bits):
    rest = [ex_bits + bit for bit in range(1, dp_bits)] + list(range(ex_bits))
    turns = [[0, 1, 2], [1, 2, 0], [2, 0, 1], [1, 0, 2]]
    orders = []
    for turn in turns:
        head = [rest[at] for at in turn if at < len(rest)]
        orders.append([ex_bits] + head + rest[len(head) :])
    return orders


def halving_kernel(n_dp, n_ex, n_arrays, with_grads, *refs):
    ins, refs = refs[:n_arrays], refs[n_arrays:]
    acts, order_ref, fulls, refs = (
        (refs[:3], refs[3], refs[4:6], refs[6:]) if with_grads else ((), None, (), refs)
    )
    outs, refs = refs[:n_arrays], refs[n_arrays:]
    if with_grads:
        grads, full_rows, grad_rows, act_rows, full_sem, grad_sem = refs[0], *refs[-5:]
        refs = refs[1:-5]
    data, recv, load_sem, send_sem, recv_sem = refs
    me = lax.axis_index("dp") * n_ex + lax.axis_index("expert")
    bits = log2(n_dp) + log2(n_ex)
    orders = halving_orders(log2(n_dp), log2(n_ex))
    rows, part = data.shape[2:]
    splits = STREAMS // n_arrays

    for stream in range(STREAMS):
        source, at = ins[stream // splits], stream % splits
        for g in range(n_dp):

            def load(e, carry, source=source, at=at, g=g, stream=stream):
                start = pl.multiple_of(e * (rows * splits) + at * rows, rows)
                pltpu.make_async_copy(
                    source.at[pl.ds(start, rows), pl.ds(g * part, part)],
                    data.at[stream, g * n_ex + e],
                    load_sem.at[stream],
                ).start()
                return carry

            lax.fori_loop(0, n_ex, load, 0)

    for at, full in enumerate(fulls):
        pltpu.make_async_copy(full, full_rows.at[at], full_sem.at[at]).start()

    def weight_grad(k):
        if k != 1:
            at = k // 2
            pltpu.make_async_copy(fulls[at], full_rows.at[at], full_sem.at[at]).wait()
        width = full_rows.shape[-1]
        piece = min(512, width)
        act_rows[...] = dot(order_ref[...], acts[k][...], 1, 1).astype(BF16)

        def product(step, carry):
            lanes = pl.ds(pl.multiple_of(step * piece, piece), piece)
            grad_rows[k, :, lanes] = jnp.dot(
                act_rows[...], full_rows[k // 2, :, lanes], preferred_element_type=F32
            ).astype(BF16)
            return carry

        lax.fori_loop(0, width // piece, product, 0)
        pltpu.make_async_copy(grad_rows.at[k], grads.at[0, k], grad_sem.at[k]).start()

    barrier = pltpu.get_barrier_semaphore()
    for place in range(bits):
        pl.semaphore_signal(
            barrier,
            inc=1,
            device_id=peer(flip(me, place), n_ex),
            device_id_type=pl.DeviceIdType.MESH,
        )
    pl.semaphore_wait(barrier, bits)

    def block_of(stream, step, choice, sent):
        order = orders[stream]
        index = 0
        for place in order[: step + 1]:
            index = index + me // (1 << place) % 2 * (1 << place)
        if sent:
            index = flip(index, order[step])
        for bit, place in enumerate(sorted(order[step + 1 :])):
            index = index + choice // (1 << bit) % 2 * (1 << place)
        return index

    def count(step):
        return 1 << (bits - 1 - step)

    def offset(step):
        return (1 << bits) - (1 << (bits - step))

    def send(stream, step, choice):
        pltpu.make_async_remote_copy(
            src_ref=data.at[stream, block_of(stream, step, choice, True)],
            dst_ref=recv.at[stream, offset(step) + choice],
            send_sem=send_sem.at[stream, step],
            recv_sem=recv_sem.at[stream, step],
            device_id=peer(flip(me, orders[stream][step]), n_ex),
            device_id_type=pl.DeviceIdType.MESH,
        ).start()

    def region(stream, step):
        view = recv.at[stream, pl.ds(offset(step), count(step))]
        return pltpu.make_async_remote_copy(
            src_ref=view,
            dst_ref=view,
            send_sem=send_sem.at[stream, step],
            recv_sem=recv_sem.at[stream, step],
            device_id=peer(flip(me, orders[stream][step]), n_ex),
            device_id_type=pl.DeviceIdType.MESH,
        )

    def number(stream, step, choice, sent):
        order = orders[stream]
        later = sorted(order[step + 1 :])
        place = order[step + 1]
        mine = me // (1 << place) % 2
        value = (1 - mine if sent else mine) * (1 << later.index(place))
        for bit, other in enumerate(sorted(order[step + 2 :])):
            value = value + choice // (1 << bit) % 2 * (1 << later.index(other))
        return value

    for stream in range(STREAMS):
        pltpu.make_async_copy(data.at[stream], data.at[stream], load_sem.at[stream]).wait()

        def first(choice, carry, stream=stream):
            send(stream, 0, choice)
            return carry

        lax.fori_loop(0, count(0), first, 0)

    if with_grads:
        weight_grad(0)
    for step in range(bits):
        for stream in range(STREAMS):
            region(stream, step).wait_recv()
            if step == bits - 1:
                total = data[stream, me].astype(F32) + recv[stream, offset(step)].astype(F32)
                outs[stream // splits][pl.ds(stream % splits * rows, rows), :] = total.astype(BF16)
                continue
            for sent in (True, False):

                def add(choice, carry, stream=stream, step=step, sent=sent):
                    block = block_of(stream, step + 1, choice, sent)
                    slot = offset(step) + number(stream, step, choice, sent)
                    total = data[stream, block].astype(F32) + recv[stream, slot].astype(F32)
                    data[stream, block] = total.astype(BF16)
                    if sent:
                        send(stream, step + 1, choice)
                    return carry

                lax.fori_loop(0, count(step + 1), add, 0)
        if step < 2 and with_grads:
            weight_grad(step + 1)

    if with_grads:
        for k in range(3):
            pltpu.make_async_copy(grad_rows.at[k], grads.at[0, k], grad_sem.at[k]).wait()
    for step in range(bits):
        for stream in range(STREAMS):
            region(stream, step).wait_send()


def halving_sum(n_dp, n_ex, arrays, acts=(), fulls=()):
    total, width = arrays[0].shape
    tok, part, n_arrays = total // n_ex, width // n_dp, len(arrays)
    rows = tok * n_arrays // STREAMS
    blocks = n_dp * n_ex
    steps = log2(blocks)
    any_spec, vmem_spec = pl.BlockSpec(memory_space=pl.ANY), pl.BlockSpec(memory_space=pltpu.VMEM)
    out_shape = [jax.ShapeDtypeStruct((tok, part), BF16)] * n_arrays
    out_specs = [vmem_spec] * n_arrays
    scratch = [
        pltpu.VMEM((STREAMS, blocks, rows, part), BF16),
        pltpu.VMEM((STREAMS, blocks - 1, rows, part), BF16),
        pltpu.SemaphoreType.DMA((STREAMS,)),
        pltpu.SemaphoreType.DMA((STREAMS, steps)),
        pltpu.SemaphoreType.DMA((STREAMS, steps)),
    ]
    if acts:
        share = acts[0].shape[1]
        out_shape = out_shape + [jax.ShapeDtypeStruct((1, 3, share, width), BF16)]
        out_specs = out_specs + [any_spec]
        scratch = scratch + [
            pltpu.VMEM((2, total, width), BF16),
            pltpu.VMEM((3, share, width), BF16),
            pltpu.VMEM((share, total), BF16),
            pltpu.SemaphoreType.DMA((2,)),
            pltpu.SemaphoreType.DMA((3,)),
        ]
    return pl.pallas_call(
        functools.partial(halving_kernel, n_dp, n_ex, n_arrays, bool(acts)),
        out_shape=out_shape,
        in_specs=[any_spec] * n_arrays + [vmem_spec] * len(acts) + [any_spec] * len(fulls),
        out_specs=out_specs,
        scratch_shapes=scratch,
        compiler_params=pltpu.CompilerParams(
            collective_id=1, has_side_effects=True, vmem_limit_bytes=60 << 20
        ),
        name="halving_sum",
    )(*arrays, *acts, *fulls)


def flip_mask(index, mask):
    place = 0
    while mask >> place:
        if mask >> place & 1:
            index = flip(index, place)
        place += 1
    return index


def gather_plan():
    every = (3, 2, 1, 0)

    def pick(*masks):
        return [("pick", mask) for mask in masks]

    def send(mask, *turns):
        return [("send", mask, turn) for turn in turns]

    def relay(mask, *turns):
        return [("pass", mask, turn) for turn in turns]

    def shared(*masks):
        return [("share", mask) for mask in masks]

    plan = pick(5) + send(5, 3, 2) + pick(1) + send(1, *every) + pick(0) + send(0, *every)
    plan += send(5, 1, 0) + [("tokens", 1)]
    plan += pick(4) + send(4, 3, 2, 1) + pick(3) + send(3, *every) + relay(5, 3, 2)
    plan += [("tokens", 2)]
    plan += pick(7) + send(7, 3, 2) + pick(2) + send(2, *every) + relay(5, 1, 0)
    plan += [("tokens", 3)]
    plan += relay(3, *every) + pick(6) + send(4, 0) + send(6, 3, 2) + send(7, 1)
    plan += send(6, 1) + send(7, 0) + send(6, 0)
    plan += relay(4, 3, 2, 1) + relay(2, 3, 2, 1) + relay(7, 3, 2)
    plan += [("units",), ("gates",), ("tokens", 4)]
    plan += shared(1, 0, 3, 2) + [("add", 0, True)] + relay(6, 3, 2)
    plan += shared(5, 4) + [("add", 2, False)] + relay(7, 1) + relay(6, 1) + relay(7, 0)
    plan += [("add", 4, False)] + shared(7, 6) + [("add", 6, False)]
    return plan


def fused_kernel(n_dp, n_ex, *refs):
    shares, owner, table, dense, tokens, cotangent, mixed, token_grad, grads, *refs = refs
    side, full, picked, weights, pre, mult, own_acts, far_acts, *refs = refs
    data, recv, swap, relay, upper, order_ref, act_rows, grad_rows, gates, gate_col, both_col, *refs = refs
    load_sem, gate_sem, row_send, row_recv, fwd_send, fwd_recv, tok_send, tok_recv, *refs = refs
    act_sem, halve_send, halve_recv, swap_sem, out_sem, relay_send, relay_recv = refs

    row, col = lax.axis_index("dp"), lax.axis_index("expert")
    me = row * n_ex + col
    core, spot_x = row % 2, row // 2
    n_x = n_dp // 2
    chip = spot_x * n_ex + col
    block_units, feat = side.shape[1:]
    pick, share = picked.shape[2], shares.shape[2]
    padded = weights.shape[1] // (2 * n_dp)
    half_units = n_dp * padded
    width = full.shape[2]
    tok = tokens.shape[0]
    quarter = tok // n_dp
    half = full.shape[1] // 2
    dp_bits, ex_bits = log2(n_dp), log2(n_ex)
    bits = dp_bits + ex_bits
    sibling = peer(flip(me, ex_bits), n_ex)
    mesh_id = pl.DeviceIdType.MESH

    def remote(src, dst, send_sem, recv_sem, device):
        return pltpu.make_async_remote_copy(
            src_ref=src,
            dst_ref=dst,
            send_sem=send_sem,
            recv_sem=recv_sem,
            device_id=device,
            device_id_type=mesh_id,
        )

    def wait(view, sem):
        pltpu.make_async_copy(view, view, sem).wait()

    def place(at, device):
        where = device // n_ex
        start = where % 2 * half + where // 2 * (n_ex * quarter) + device % n_ex * quarter
        return full.at[at, pl.ds(pl.multiple_of(start, quarter), quarter), :]

    for at, source in enumerate((tokens, cotangent)):
        pltpu.make_async_copy(
            source.at[pl.ds(pl.multiple_of(row * quarter, quarter), quarter), :],
            place(at, me),
            load_sem.at[at],
        ).start()
    pltpu.make_async_copy(dense, side, load_sem.at[2]).start()
    pltpu.make_async_copy(table.at[col], gates.at[col], gate_sem.at[1]).start()

    if padded > pick:
        for k in range(3):
            for slot in range(2 * n_dp):
                rows = pl.ds(slot * padded + pick, padded - pick)
                weights[k, rows, :] = jnp.zeros((padded - pick, width), BF16)

    barrier = pltpu.get_barrier_semaphore()
    for mask in range(1, n_dp * n_ex):
        pl.semaphore_signal(
            barrier, inc=1, device_id=peer(flip_mask(me, mask), n_ex), device_id_type=mesh_id
        )
    upper[...] = (
        lax.broadcasted_iota(jnp.int32, (share, share), 0)
        < lax.broadcasted_iota(jnp.int32, (share, share), 1)
    ).astype(BF16)
    pl.semaphore_wait(barrier, n_dp * n_ex - 1)

    for at in range(2):
        wait(place(at, me), load_sem.at[at])

    ex_order = list(range(ex_bits - 1, -1, -1))
    dp_order = [ex_bits + bit for bit in range(dp_bits - 1, -1, -1)]
    tok_orders = [
        ex_order + dp_order,
        ex_order[:-1] + [dp_order[0], ex_order[-1]] + dp_order[1:],
    ]

    def send_tokens(step):
        for at in range(2):
            order = tok_orders[at]

            def one(choice, carry, at=at, order=order):
                device = me
                for bit, other in enumerate(order[:step]):
                    mine = me // (1 << other) % 2
                    device = device + (choice // (1 << bit) % 2 - mine) * (1 << other)
                remote(
                    place(at, device),
                    place(at, device),
                    tok_send.at[at, step],
                    tok_recv.at[at, step],
                    peer(flip(me, order[step]), n_ex),
                ).start()
                return carry

            lax.fori_loop(0, 1 << step, one, 0)

    def wait_tokens(step, sem):
        for at in range(2):
            wait(full.at[at, pl.ds(0, (1 << step) * quarter), :], sem.at[at, step])

    send_tokens(0)
    for mask in range(1, n_ex):
        device = flip_mask(me, mask)
        remote(
            table.at[device % n_ex],
            gates.at[col],
            gate_sem.at[0],
            gate_sem.at[1],
            peer(device, n_ex),
        ).start()
    wait(side, load_sem.at[2])

    def ranks(mask):
        return jnp.dot(mask.astype(BF16), upper[...], preferred_element_type=F32)

    def pick_rows(mask):
        target = flip_mask(col, mask)
        local = shares[owner[target]] - row * block_units
        inside = jnp.logical_and(local >= 0, local < block_units)
        spots = jnp.where(inside, ranks(inside), -1.0)
        values = (local + 1).astype(F32)
        hots = []
        for g in range(n_dp):
            hit = spots[g : g + 1, :] == lax.broadcasted_iota(
                jnp.int32, (padded, share), 0
            ).astype(F32)
            units = jnp.sum(jnp.where(hit, values[g : g + 1, :], 0.0), axis=1, keepdims=True)
            hots.append(
                (
                    units.astype(jnp.int32) - 1
                    == lax.broadcasted_iota(jnp.int32, (padded, block_units), 1)
                ).astype(BF16)
            )
        hot = jnp.concatenate(hots, axis=0)
        for k in range(3):
            rows = jnp.dot(hot, side[k], preferred_element_type=F32).astype(BF16)
            for g in range(n_dp):
                picked[mask * n_dp + g, k] = rows[g * padded : g * padded + pick, :]

    def spot_of(holder, g, source_col):
        start = pl.multiple_of((g % 2 * n_dp + holder) * padded, padded)
        return weights.at[
            :, pl.ds(start, pick), pl.ds(pl.multiple_of(source_col * feat, feat), feat)
        ]

    def send_rows(mask, turn):
        z_mask, slot = mask // 2, mask % 2 * n_dp + turn
        g = flip_mask(row, turn)
        source = picked.at[mask * n_dp + g]
        if mask == 0 and turn == 0:
            pltpu.make_async_copy(source, spot_of(row, row, col), row_recv.at[col]).start()
        elif z_mask and slot:
            remote(
                source,
                relay.at[z_mask - 1, slot - 1],
                row_send.at[0],
                relay_recv.at[z_mask - 1, slot - 1],
                {"dp": row, "expert": flip_mask(col, 2 * z_mask)},
            ).start()
        else:
            remote(
                source,
                spot_of(row, g, col),
                row_send.at[0],
                row_recv.at[col],
                {"dp": g, "expert": flip_mask(col, mask)},
            ).start()

    def pass_rows(mask, turn):
        z_mask, slot = mask // 2, mask % 2 * n_dp + turn
        source = relay.at[z_mask - 1, slot - 1]
        source_col = flip_mask(col, 2 * z_mask)
        g = flip_mask(row, turn)
        wait(source, relay_recv.at[z_mask - 1, slot - 1])
        remote(
            source,
            spot_of(row, g, source_col),
            relay_send.at[0],
            row_recv.at[source_col],
            {"dp": g, "expert": flip_mask(col, mask % 2)},
        ).start()

    def step_tokens(step):
        wait_tokens(step - 1, tok_recv)
        send_tokens(step)

    def place_units():
        mine = shares[owner[col], pl.ds(row, 1), :]
        at_row = jnp.zeros((1, share), F32)
        for b in range(n_dp):
            inside = jnp.logical_and(mine >= b * block_units, mine < (b + 1) * block_units)
            at_row = at_row + jnp.where(inside, ranks(inside) + float(b * padded), 0.0)
        diagonal = lax.broadcasted_iota(jnp.int32, (share, share), 0) == lax.broadcasted_iota(
            jnp.int32, (share, share), 1
        )
        at_col = jnp.sum(jnp.where(diagonal, at_row, 0.0), axis=1, keepdims=True)
        order_ref[...] = (
            at_col.astype(jnp.int32) == lax.broadcasted_iota(jnp.int32, (share, half_units), 1)
        ).astype(BF16)

    def place_gates():
        wait(table.at[pl.ds(0, n_ex - 1)], gate_sem.at[0])
        wait(gates, gate_sem.at[1])
        copy_id = owner[col] // (n_ex // 2)
        lanes = lax.broadcasted_iota(jnp.int32, (quarter, tok), 1)
        below = lax.broadcasted_iota(jnp.int32, (quarter, tok), 0)
        for xq in range(n_x):

            def column(block, carry, xq=xq):
                hit = lanes == below + (xq * 2 + core) * quarter
                value = jnp.sum(jnp.where(hit, gates[block], 0.0), axis=1, keepdims=True)
                value = jnp.broadcast_to(value, (quarter, 128))
                blocks = jnp.full((quarter, 128), block * 2 // n_ex, jnp.int32)
                rows = pl.ds(pl.multiple_of((xq * n_ex + block) * quarter, quarter), quarter)
                gate_col[rows, :] = value
                both_col[rows, :] = value + (blocks == copy_id).astype(F32)
                return carry

            lax.fori_loop(0, n_ex, column, 0)

    my_rows = pl.ds(pl.multiple_of(core * half, half), half)
    my_units = pl.ds(pl.multiple_of(core * half_units, half_units), half_units)
    far_units = pl.ds(pl.multiple_of((1 - core) * half_units, half_units), half_units)
    n_tile = min(256, 2 * half_units)
    tiles = 2 * half_units // n_tile

    def columns(mask):
        return pl.ds(pl.multiple_of(flip_mask(col, mask) * feat, feat), feat)

    def forward(mask):
        f = flip_mask(col, mask)
        count = n_dp * pick
        wait(weights.at[:, pl.ds(0, count), columns(mask)], row_recv.at[f])
        for k in range(3):
            view = weights.at[k, my_units, columns(mask)]
            remote(view, view, fwd_send.at[0], fwd_recv.at[f], sibling).start()

    def accumulate(mask, first):
        for near in range(2):
            f = flip_mask(col, mask + near)
            wait(weights.at[:, far_units, columns(mask + near)], fwd_recv.at[f])
        both = pl.ds(pl.multiple_of(flip_mask(col, mask) // 2 * (2 * feat), 2 * feat), 2 * feat)

        def one(index, carry):
            k, n = index // tiles, index % tiles
            units = pl.ds(pl.multiple_of(n * n_tile, n_tile), n_tile)
            value = dot(full[k // 2, my_rows, both], weights[k, units, both], 1, 1)
            if first:
                pre[k, :, units] = value
            else:
                pre[k, :, units] = pre[k, :, units] + value
            return carry

        lax.fori_loop(0, 3 * tiles, one, 0)

    acts = {
        "pick": pick_rows,
        "send": send_rows,
        "pass": pass_rows,
        "tokens": step_tokens,
        "units": place_units,
        "gates": place_gates,
        "share": forward,
        "add": accumulate,
    }
    for name, *where in gather_plan():
        acts[name](*where)

    r_tile = 32

    def activate(share_at, keep):
        units = pl.ds(pl.multiple_of(share_at * half_units, half_units), half_units)

        def one(index, carry):
            rows = pl.ds(pl.multiple_of(index * r_tile, r_tile), r_tile)
            reps = (1, half_units // 128)
            gate = jnp.tile(gate_col[rows, :], reps)
            both = jnp.tile(both_col[rows, :], reps)
            act, slope = silu_parts(pre[0, rows, units])
            up, d_hidden = pre[1, rows, units], pre[2, rows, units]
            values = (d_hidden * up * slope, d_hidden * act, act * up)
            for k, value in enumerate(values):
                mult[k, rows, units] = (both * value).astype(BF16)
                if keep:
                    own_acts[core, k, rows, :] = (gate * value).astype(BF16)
                else:
                    far_acts[k, rows, :] = (gate * value).astype(BF16)
            return carry

        lax.fori_loop(0, half // r_tile, one, 0)

    activate(1 - core, False)
    act_copy = remote(far_acts, own_acts.at[core], act_sem.at[0], act_sem.at[1], sibling)
    act_copy.start()
    activate(core, True)

    chip_bits = bits - 1
    x_place, y_place, z_low = chip_bits - 1, 0, 1
    rest = list(range(2, chip_bits - 1))
    classes = {
        "a": [x_place, y_place, z_low] + rest,
        "b": [y_place, z_low, x_place] + rest,
        "c": [z_low, x_place, y_place] + rest,
    }
    kinds = ["a", "a", "a", "c", "b", "b", "b", "c"]
    turns = [0, 4, 3, 1, 5, 7, 2, 6]
    chunk = data.shape[3]
    per_array = width // n_x // chunk
    r_rows = data.shape[2]

    def chip_peer(place_at):
        if place_at == x_place:
            return peer(flip(me, bits - 1), n_ex)
        return peer(flip(me, place_at), n_ex)

    def block_of(stream, step, choice, sent):
        order = classes[kinds[stream]]
        index = 0
        for place_at in order[: step + 1]:
            index = index + chip // (1 << place_at) % 2 * (1 << place_at)
        if sent:
            index = flip(index, order[step])
        for bit, place_at in enumerate(sorted(order[step + 1 :])):
            index = index + choice // (1 << bit) % 2 * (1 << place_at)
        return index

    def count(step):
        return 1 << (chip_bits - 1 - step)

    def offset(step):
        return (1 << chip_bits) - (1 << (chip_bits - step))

    def send(stream, step, choice):
        remote(
            data.at[stream, block_of(stream, step, choice, True)],
            recv.at[stream, offset(step) + choice],
            halve_send.at[stream, step],
            halve_recv.at[stream, step],
            chip_peer(classes[kinds[stream]][step]),
        ).start()

    def region(stream, step):
        return recv.at[stream, pl.ds(offset(step), count(step))]

    def number(stream, step, choice, sent):
        order = classes[kinds[stream]]
        later = sorted(order[step + 1 :])
        place_at = order[step + 1]
        mine_bit = chip // (1 << place_at) % 2
        value = (1 - mine_bit if sent else mine_bit) * (1 << later.index(place_at))
        for bit, other in enumerate(sorted(order[step + 2 :])):
            value = value + choice // (1 << bit) % 2 * (1 << later.index(other))
        return value

    def product(stream, xq):
        array, j = stream // per_array, stream % per_array
        cols = pl.ds(pl.multiple_of(xq * (width // n_x) + j * chunk, chunk), chunk)
        if array == 0:
            value = jnp.dot(mult[2], weights[2, :, cols], preferred_element_type=F32)
        else:
            value = jnp.dot(mult[0], weights[0, :, cols], preferred_element_type=F32)
            value = value + jnp.dot(mult[1], weights[1, :, cols], preferred_element_type=F32)
        value = value.astype(BF16).reshape(n_x, n_ex, quarter, chunk)
        for part in range(n_x):
            data[
                stream,
                pl.ds(pl.multiple_of(xq * n_ex, n_ex), n_ex),
                part * quarter : (part + 1) * quarter,
                :,
            ] = value[part]

    def begin(stream):
        def first(choice, carry):
            send(stream, 0, choice)
            return carry

        lax.fori_loop(0, count(0), first, 0)

    for stream in turns:
        if kinds[stream] == "a":
            product(stream, 1 - spot_x)
            begin(stream)
        else:

            def both_sides(side_at, carry, stream=stream):
                product(stream, side_at)
                return carry

            lax.fori_loop(0, n_x, both_sides, 0)
            begin(stream)
    for stream in turns:
        if kinds[stream] == "a":
            product(stream, spot_x)

    def weight_grad(k):
        for part in range(2):
            act_rows[:, part * half : (part + 1) * half] = dot(
                order_ref[...], own_acts[part, k], 1, 1
            ).astype(BF16)
        piece = min(512, width)

        def one(step, carry):
            where = pl.ds(pl.multiple_of(step * piece, piece), piece)
            grad_rows[k, :, where] = jnp.dot(
                act_rows[...], full[k // 2, :, where], preferred_element_type=F32
            ).astype(BF16)
            return carry

        lax.fori_loop(0, width // piece, one, 0)
        pltpu.make_async_copy(grad_rows.at[k], grads.at[0, k], out_sem.at[k]).start()

    def combine(stream, step):
        wait(region(stream, step), halve_recv.at[stream, step])
        for sent in (True, False):

            def add(choice, carry, sent=sent):
                block = block_of(stream, step + 1, choice, sent)
                slot = offset(step) + number(stream, step, choice, sent)
                total = data[stream, block].astype(F32) + recv[stream, slot].astype(F32)
                data[stream, block] = total.astype(BF16)
                if sent:
                    send(stream, step + 1, choice)
                return carry

            lax.fori_loop(0, count(step + 1), add, 0)

    wait_tokens(bits - 1, tok_recv)
    act_copy.wait()
    fill = {(0, 0): 0, (0, 3): 1, (0, 6): 2}
    for step in range(chip_bits - 1):
        for at, stream in enumerate(turns):
            if (step, at) in fill:
                weight_grad(fill[step, at])
            combine(stream, step)

    last = chip_bits - 1
    results = (mixed, token_grad)

    def finish(array, i, keep):
        owner_core = core if keep else 1 - core
        stream = array * per_array + owner_core * (per_array // 2) + i
        wait(recv.at[stream, pl.ds(offset(last), 1)], halve_recv.at[stream, last])
        total = (
            data[stream, chip].astype(F32) + recv[stream, offset(last)].astype(F32)
        ).astype(BF16)
        if keep:
            put(array, i, core, total)
        else:
            data[stream, chip] = total
            remote(
                data.at[stream, chip],
                swap.at[array, i],
                swap_sem.at[0],
                swap_sem.at[1],
                sibling,
            ).start()

    def put(array, i, which, total):
        for part in range(n_x):
            start = pl.multiple_of((part * 2 + which) * quarter, quarter)
            results[array][pl.ds(start, quarter), i * chunk : (i + 1) * chunk] = total[
                part * quarter : (part + 1) * quarter
            ]

    for keep in (False, True):
        for array in range(2):
            for i in range(per_array // 2):
                finish(array, i, keep)
    wait(swap, swap_sem.at[1])
    for array in range(2):
        for i in range(per_array // 2):
            put(array, i, 1 - core, swap[array, i])

    for k in range(3):
        pltpu.make_async_copy(grad_rows.at[k], grads.at[0, k], out_sem.at[k]).wait()
    wait(picked.at[pl.ds(0, n_dp * n_ex - 1)], row_send.at[0])
    wait(relay, relay_send.at[0])
    wait(weights.at[:, my_units, :], fwd_send.at[0])
    for step in range(bits):
        wait_tokens(step, tok_send)
    for step in range(chip_bits):
        for stream in range(len(kinds)):
            wait(region(stream, step), halve_send.at[stream, step])
    wait(swap, swap_sem.at[0])


def fused_step(n_dp, n_ex, shares, slab_owner, table, dense_weights, tokens, cotangent):
    _, block_units, feat = dense_weights.shape
    tok, width = tokens.shape
    share = shares.shape[2]
    pick = share // n_dp
    padded = -(-pick // 16) * 16
    half_units, half = n_dp * padded, n_ex * tok // 2
    blocks, bits, n_x = n_dp * n_ex, log2(n_dp * n_ex), n_dp // 2
    chips, chunk = blocks // 2, 256
    streams = 2 * (width // n_x // chunk)
    any_spec, vmem_spec = pl.BlockSpec(memory_space=pl.ANY), pl.BlockSpec(memory_space=pltpu.VMEM)
    r_rows = tok // 2
    return pl.pallas_call(
        functools.partial(fused_kernel, n_dp, n_ex),
        out_shape=[
            jax.ShapeDtypeStruct((tok, width // n_dp), BF16),
            jax.ShapeDtypeStruct((tok, width // n_dp), BF16),
            jax.ShapeDtypeStruct((1, 3, share, width), BF16),
        ],
        in_specs=[
            vmem_spec,
            pl.BlockSpec(memory_space=pltpu.SMEM),
            vmem_spec,
            any_spec,
            any_spec,
            any_spec,
        ],
        out_specs=[vmem_spec, vmem_spec, any_spec],
        scratch_shapes=[
            pltpu.VMEM((3, block_units, feat), BF16),
            pltpu.VMEM((2, n_ex * tok, width), BF16),
            pltpu.VMEM((blocks, 3, pick, feat), BF16),
            pltpu.VMEM((3, 2 * half_units, width), BF16),
            pltpu.VMEM((3, half, 2 * half_units), F32),
            pltpu.VMEM((3, half, 2 * half_units), BF16),
            pltpu.VMEM((2, 3, half, half_units), BF16),
            pltpu.VMEM((3, half, half_units), BF16),
            pltpu.VMEM((streams, chips, r_rows, chunk), BF16),
            pltpu.VMEM((streams, chips - 1, r_rows, chunk), BF16),
            pltpu.VMEM((2, streams // 4, r_rows, chunk), BF16),
            pltpu.VMEM((n_ex // 2 - 1, 2 * n_dp - 1, 3, pick, feat), BF16),
            pltpu.VMEM((share, share), BF16),
            pltpu.VMEM((share, half_units), BF16),
            pltpu.VMEM((share, n_ex * tok), BF16),
            pltpu.VMEM((3, share, width), BF16),
            pltpu.VMEM((n_ex, 1, tok), F32),
            pltpu.VMEM((half, 128), F32),
            pltpu.VMEM((half, 128), F32),
            pltpu.SemaphoreType.DMA((3,)),
            pltpu.SemaphoreType.DMA((2,)),
            pltpu.SemaphoreType.DMA((1,)),
            pltpu.SemaphoreType.DMA((n_ex,)),
            pltpu.SemaphoreType.DMA((1,)),
            pltpu.SemaphoreType.DMA((n_ex,)),
            pltpu.SemaphoreType.DMA((2, bits)),
            pltpu.SemaphoreType.DMA((2, bits)),
            pltpu.SemaphoreType.DMA((2,)),
            pltpu.SemaphoreType.DMA((streams, bits - 1)),
            pltpu.SemaphoreType.DMA((streams, bits - 1)),
            pltpu.SemaphoreType.DMA((2,)),
            pltpu.SemaphoreType.DMA((3,)),
            pltpu.SemaphoreType.DMA((1,)),
            pltpu.SemaphoreType.DMA((n_ex // 2 - 1, 2 * n_dp - 1)),
        ],
        compiler_params=pltpu.CompilerParams(
            collective_id=2, has_side_effects=True, vmem_limit_bytes=63 << 20
        ),
        name="fused_step",
    )(shares, slab_owner, table.reshape(n_ex, 1, tok), dense_weights, tokens, cotangent)


def gather_plain(n_dp, n_ex, row, picked, tokens, cotangent, table):
    _, pick, wide = picked.shape
    tok, width = tokens.shape
    arrived = lax.all_to_all(picked, ("dp", "expert"), split_axis=0, concat_axis=0, tiled=True)
    arrived = arrived.reshape(n_dp, n_ex, pick, 3, wide // 3)
    weights = jnp.transpose(arrived, (3, 0, 2, 1, 4)).reshape(3, n_dp * pick, width)
    part = width // n_dp
    both = jnp.concatenate(
        [
            lax.dynamic_slice(tokens, (0, row * part), (tok, part)),
            lax.dynamic_slice(cotangent, (0, row * part), (tok, part)),
        ],
        axis=1,
    )
    both = lax.all_gather(both, "expert", axis=0, tiled=True)
    both = lax.all_gather(both, "dp", axis=0, tiled=False)
    all_x = jnp.transpose(both[:, :, :part], (1, 0, 2)).reshape(n_ex * tok, width)
    all_c = jnp.transpose(both[:, :, part:], (1, 0, 2)).reshape(n_ex * tok, width)
    gates = lax.all_to_all(table, "expert", split_axis=0, concat_axis=0, tiled=True)
    return weights, all_x, all_c, gates


def body(dense_weights, tokens, cotangent, routes, route_gates, unit_perm, slab_owner):
    n_dp = lax.axis_size("dp")
    n_ex = lax.axis_size("expert")
    row = lax.axis_index("dp")
    col = lax.axis_index("expert")
    _, block_units, feat = dense_weights.shape
    copies, total_units = unit_perm.shape
    slabs = n_ex // copies
    slab_units = total_units // slabs
    share = slab_units // n_dp
    pick = share // n_dp
    tok, width = tokens.shape

    shares = unit_perm.reshape(n_ex, n_dp, share)
    gate_table = jnp.sum(
        jnp.where(
            routes[None, :, :] == lax.broadcasted_iota(jnp.int32, (n_ex, 1, 1), 0),
            route_gates[None, :, :],
            0.0,
        ),
        axis=2,
    )
    padded = -(-pick // 16) * 16
    if (
        copies == 2
        and pick % 8 == 0
        and feat % 256 == 0
        and n_dp * padded % 128 == 0
        and 2 * n_dp * padded % 256 == 0
        and n_dp == 4
        and n_ex == 8
        and width == n_dp * 512
        and tok == 128
    ):
        return tuple(
            fused_step(
                n_dp, n_ex, shares, slab_owner, gate_table, dense_weights, tokens, cotangent
            )
        )
    dest = jnp.transpose(shares[slab_owner], (1, 0, 2)).reshape(n_dp * n_ex, share)
    mask, rank = block_ranks(dest // block_units, row)
    place = jnp.where(mask, rank, -1)
    hit = place[:, None, :] == lax.broadcasted_iota(jnp.int32, (1, pick, 1), 1)
    units = jnp.sum(jnp.where(hit, (dest - row * block_units)[:, None, :], 0), axis=2)
    onehot = (
        units.reshape(-1, 1) == lax.broadcasted_iota(jnp.int32, (1, block_units), 1)
    ).astype(BF16)
    side = jnp.concatenate([dense_weights[0], dense_weights[1], dense_weights[2]], axis=1)
    picked = dot(onehot, side, 1, 0).astype(BF16)
    picked = picked.reshape(n_dp * n_ex, pick, 3 * feat)
    mine = lax.dynamic_slice(
        shares, (slab_owner[col], row, 0), (1, 1, share)
    ).reshape(1, share)
    mine_block = mine // block_units
    mask, rank = block_ranks(
        jnp.broadcast_to(mine_block, (n_dp, share)),
        lax.broadcasted_iota(jnp.int32, (n_dp, 1), 0),
    )
    at = jnp.sum(
        jnp.where(mask, rank + lax.broadcasted_iota(jnp.int32, (n_dp, 1), 0) * pick, 0), axis=0
    )
    order = (lax.broadcasted_iota(jnp.int32, (share, share), 1) == at[:, None]).astype(BF16)

    weights, all_x, all_c, gate = gather_plain(
        n_dp, n_ex, row, picked, tokens, cotangent, gate_table
    )
    w_gate, w_up, w_down = weights[0], weights[1], weights[2]
    gate = gate.reshape(n_ex * tok, 1)
    copy_id = slab_owner[col] // slabs
    owner_block = lax.broadcasted_iota(jnp.int32, (n_ex, tok), 0).reshape(n_ex * tok, 1)
    both_weight = gate + (owner_block * copies // n_ex == copy_id).astype(F32)

    pre_gate = dot(all_x, w_gate, 1, 1)
    pre_up = dot(all_x, w_up, 1, 1)
    d_hidden = dot(all_c, w_down, 1, 1)
    act, slope = silu_parts(pre_gate)
    hidden = act * pre_up
    d_gate = d_hidden * pre_up * slope
    d_up = d_hidden * act

    out = dot((both_weight * hidden).astype(BF16), w_down, 1, 0).astype(BF16)
    back = (
        dot((both_weight * d_gate).astype(BF16), w_gate, 1, 0)
        + dot((both_weight * d_up).astype(BF16), w_up, 1, 0)
    ).astype(BF16)

    acts = [(gate * values).astype(BF16) for values in (d_gate, d_up, hidden)]
    if out.size * out.dtype.itemsize <= 1 << 23:
        mixed, token_grad, weight_grads = halving_sum(
            n_dp, n_ex, [out, back], acts + [order], [all_x, all_c]
        )
    else:
        acts = [dot(order, values, 1, 1).astype(BF16) for values in acts]
        weight_grads = jnp.stack(
            [dot(acts[0], all_x, 1, 0), dot(acts[1], all_x, 1, 0), dot(acts[2], all_c, 1, 0)]
        ).astype(BF16)[None]
        (mixed,) = halving_sum(n_dp, n_ex, [out])
        (token_grad,) = halving_sum(n_dp, n_ex, [back])
    return (mixed, token_grad, weight_grads)


def solution(mesh):
    in_specs = (
        P(None, "dp", "expert"),
        P("expert", None),
        P("expert", None),
        P("expert", None),
        P("expert", None),
        P(),
        P(),
    )
    out_specs = (P("expert", "dp"), P("expert", "dp"), P("expert", None, "dp", None))
    return jax.shard_map(body, mesh=mesh, in_specs=in_specs, out_specs=out_specs, check_vma=False)
```

```python
import functools

import jax
import jax.numpy as jnp
from jax import lax
from jax.experimental import pallas as pl
from jax.experimental.pallas import tpu as pltpu
from jax.sharding import PartitionSpec as P

F32 = jnp.float32
BF16 = jnp.bfloat16


def silu_parts(preact):
    sigmoid_value = jax.nn.sigmoid(preact)
    return (preact * sigmoid_value, sigmoid_value * (1.0 + preact * (1.0 - sigmoid_value)))


def dot(left, right, left_dim, right_dim):
    return lax.dot_general(
        left, right, (((left_dim,), (right_dim,)), ((), ())), preferred_element_type=F32
    )


def block_ranks(blocks, block):
    width = blocks.shape[-1]
    mask = blocks == block
    upper = lax.broadcasted_iota(jnp.int32, (width, width), 0) < lax.broadcasted_iota(
        jnp.int32, (width, width), 1
    )
    rank = jnp.dot(mask.astype(BF16), upper.astype(BF16), preferred_element_type=F32)
    return mask, rank.astype(jnp.int32)


def log2(count):
    return count.bit_length() - 1


def flip(index, place):
    return index + (1 - 2 * (index // (1 << place) % 2)) * (1 << place)


def peer(device, n_ex):
    return {"dp": device // n_ex, "expert": device % n_ex}


STREAMS = 4


def halving_orders(dp_bits, ex_bits):
    rest = [ex_bits + bit for bit in range(1, dp_bits)] + list(range(ex_bits))
    turns = [[0, 1, 2], [1, 2, 0], [2, 0, 1], [1, 0, 2]]
    orders = []
    for turn in turns:
        head = [rest[at] for at in turn if at < len(rest)]
        orders.append([ex_bits] + head + rest[len(head) :])
    return orders


def halving_kernel(n_dp, n_ex, n_arrays, with_grads, *refs):
    ins, refs = refs[:n_arrays], refs[n_arrays:]
    acts, order_ref, fulls, refs = (
        (refs[:3], refs[3], refs[4:6], refs[6:]) if with_grads else ((), None, (), refs)
    )
    outs, refs = refs[:n_arrays], refs[n_arrays:]
    if with_grads:
        grads, full_rows, grad_rows, act_rows, full_sem, grad_sem = refs[0], *refs[-5:]
        refs = refs[1:-5]
    data, recv, load_sem, send_sem, recv_sem = refs
    me = lax.axis_index("dp") * n_ex + lax.axis_index("expert")
    bits = log2(n_dp) + log2(n_ex)
    orders = halving_orders(log2(n_dp), log2(n_ex))
    rows, part = data.shape[2:]
    splits = STREAMS // n_arrays

    for stream in range(STREAMS):
        source, at = ins[stream // splits], stream % splits
        for g in range(n_dp):

            def load(e, carry, source=source, at=at, g=g, stream=stream):
                start = pl.multiple_of(e * (rows * splits) + at * rows, rows)
                pltpu.make_async_copy(
                    source.at[pl.ds(start, rows), pl.ds(g * part, part)],
                    data.at[stream, g * n_ex + e],
                    load_sem.at[stream],
                ).start()
                return carry

            lax.fori_loop(0, n_ex, load, 0)

    for at, full in enumerate(fulls):
        pltpu.make_async_copy(full, full_rows.at[at], full_sem.at[at]).start()

    def weight_grad(k):
        if k != 1:
            at = k // 2
            pltpu.make_async_copy(fulls[at], full_rows.at[at], full_sem.at[at]).wait()
        width = full_rows.shape[-1]
        piece = min(512, width)
        act_rows[...] = dot(order_ref[...], acts[k][...], 1, 1).astype(BF16)

        def product(step, carry):
            lanes = pl.ds(pl.multiple_of(step * piece, piece), piece)
            grad_rows[k, :, lanes] = jnp.dot(
                act_rows[...], full_rows[k // 2, :, lanes], preferred_element_type=F32
            ).astype(BF16)
            return carry

        lax.fori_loop(0, width // piece, product, 0)
        pltpu.make_async_copy(grad_rows.at[k], grads.at[0, k], grad_sem.at[k]).start()

    barrier = pltpu.get_barrier_semaphore()
    for place in range(bits):
        pl.semaphore_signal(
            barrier,
            inc=1,
            device_id=peer(flip(me, place), n_ex),
            device_id_type=pl.DeviceIdType.MESH,
        )
    pl.semaphore_wait(barrier, bits)

    def block_of(stream, step, choice, sent):
        order = orders[stream]
        index = 0
        for place in order[: step + 1]:
            index = index + me // (1 << place) % 2 * (1 << place)
        if sent:
            index = flip(index, order[step])
        for bit, place in enumerate(sorted(order[step + 1 :])):
            index = index + choice // (1 << bit) % 2 * (1 << place)
        return index

    def count(step):
        return 1 << (bits - 1 - step)

    def offset(step):
        return (1 << bits) - (1 << (bits - step))

    def send(stream, step, choice):
        pltpu.make_async_remote_copy(
            src_ref=data.at[stream, block_of(stream, step, choice, True)],
            dst_ref=recv.at[stream, offset(step) + choice],
            send_sem=send_sem.at[stream, step],
            recv_sem=recv_sem.at[stream, step],
            device_id=peer(flip(me, orders[stream][step]), n_ex),
            device_id_type=pl.DeviceIdType.MESH,
        ).start()

    def region(stream, step):
        view = recv.at[stream, pl.ds(offset(step), count(step))]
        return pltpu.make_async_remote_copy(
            src_ref=view,
            dst_ref=view,
            send_sem=send_sem.at[stream, step],
            recv_sem=recv_sem.at[stream, step],
            device_id=peer(flip(me, orders[stream][step]), n_ex),
            device_id_type=pl.DeviceIdType.MESH,
        )

    def number(stream, step, choice, sent):
        order = orders[stream]
        later = sorted(order[step + 1 :])
        place = order[step + 1]
        mine = me // (1 << place) % 2
        value = (1 - mine if sent else mine) * (1 << later.index(place))
        for bit, other in enumerate(sorted(order[step + 2 :])):
            value = value + choice // (1 << bit) % 2 * (1 << later.index(other))
        return value

    for stream in range(STREAMS):
        pltpu.make_async_copy(data.at[stream], data.at[stream], load_sem.at[stream]).wait()

        def first(choice, carry, stream=stream):
            send(stream, 0, choice)
            return carry

        lax.fori_loop(0, count(0), first, 0)

    if with_grads:
        weight_grad(0)
    for step in range(bits):
        for stream in range(STREAMS):
            region(stream, step).wait_recv()
            if step == bits - 1:
                total = data[stream, me].astype(F32) + recv[stream, offset(step)].astype(F32)
                outs[stream // splits][pl.ds(stream % splits * rows, rows), :] = total.astype(BF16)
                continue
            for sent in (True, False):

                def add(choice, carry, stream=stream, step=step, sent=sent):
                    block = block_of(stream, step + 1, choice, sent)
                    slot = offset(step) + number(stream, step, choice, sent)
                    total = data[stream, block].astype(F32) + recv[stream, slot].astype(F32)
                    data[stream, block] = total.astype(BF16)
                    if sent:
                        send(stream, step + 1, choice)
                    return carry

                lax.fori_loop(0, count(step + 1), add, 0)
        if step < 2 and with_grads:
            weight_grad(step + 1)

    if with_grads:
        for k in range(3):
            pltpu.make_async_copy(grad_rows.at[k], grads.at[0, k], grad_sem.at[k]).wait()
    for step in range(bits):
        for stream in range(STREAMS):
            region(stream, step).wait_send()


def halving_sum(n_dp, n_ex, arrays, acts=(), fulls=()):
    total, width = arrays[0].shape
    tok, part, n_arrays = total // n_ex, width // n_dp, len(arrays)
    rows = tok * n_arrays // STREAMS
    blocks = n_dp * n_ex
    steps = log2(blocks)
    any_spec, vmem_spec = pl.BlockSpec(memory_space=pl.ANY), pl.BlockSpec(memory_space=pltpu.VMEM)
    out_shape = [jax.ShapeDtypeStruct((tok, part), BF16)] * n_arrays
    out_specs = [vmem_spec] * n_arrays
    scratch = [
        pltpu.VMEM((STREAMS, blocks, rows, part), BF16),
        pltpu.VMEM((STREAMS, blocks - 1, rows, part), BF16),
        pltpu.SemaphoreType.DMA((STREAMS,)),
        pltpu.SemaphoreType.DMA((STREAMS, steps)),
        pltpu.SemaphoreType.DMA((STREAMS, steps)),
    ]
    if acts:
        share = acts[0].shape[1]
        out_shape = out_shape + [jax.ShapeDtypeStruct((1, 3, share, width), BF16)]
        out_specs = out_specs + [any_spec]
        scratch = scratch + [
            pltpu.VMEM((2, total, width), BF16),
            pltpu.VMEM((3, share, width), BF16),
            pltpu.VMEM((share, total), BF16),
            pltpu.SemaphoreType.DMA((2,)),
            pltpu.SemaphoreType.DMA((3,)),
        ]
    return pl.pallas_call(
        functools.partial(halving_kernel, n_dp, n_ex, n_arrays, bool(acts)),
        out_shape=out_shape,
        in_specs=[any_spec] * n_arrays + [vmem_spec] * len(acts) + [any_spec] * len(fulls),
        out_specs=out_specs,
        scratch_shapes=scratch,
        compiler_params=pltpu.CompilerParams(
            collective_id=1, has_side_effects=True, vmem_limit_bytes=60 << 20
        ),
        name="halving_sum",
    )(*arrays, *acts, *fulls)


def flip_mask(index, mask):
    place = 0
    while mask >> place:
        if mask >> place & 1:
            index = flip(index, place)
        place += 1
    return index


def gather_plan():
    every = (3, 2, 1, 0)

    def pick(*masks):
        return [("pick", mask) for mask in masks]

    def send(mask, *turns):
        return [("send", mask, turn) for turn in turns]

    def relay(mask, *turns):
        return [("pass", mask, turn) for turn in turns]

    def shared(*masks):
        return [("share", mask) for mask in masks]

    plan = pick(5) + send(5, 3, 2) + pick(1) + send(1, *every) + pick(0) + send(0, *every)
    plan += send(5, 1, 0) + [("tokens", 1)]
    plan += pick(4) + send(4, 3, 2, 1) + pick(3) + send(3, *every) + relay(5, 3, 2)
    plan += [("tokens", 2)]
    plan += pick(7) + send(7, 3, 2) + pick(2) + send(2, *every) + relay(5, 1, 0)
    plan += [("tokens", 3)]
    plan += relay(3, *every) + pick(6) + send(4, 0) + send(6, 3, 2) + send(7, 1)
    plan += send(6, 1) + send(7, 0) + send(6, 0)
    plan += relay(4, 3, 2, 1) + relay(2, 3, 2, 1) + relay(7, 3, 2)
    plan += [("units",), ("gates",), ("tokens", 4)]
    plan += shared(1, 0, 3, 2) + [("add", 0, True)] + relay(6, 3, 2)
    plan += shared(5, 4) + [("add", 2, False)] + relay(7, 1) + relay(6, 1) + relay(7, 0)
    plan += [("add", 4, False)] + shared(7, 6) + [("add", 6, False)]
    return plan


def fused_kernel(n_dp, n_ex, *refs):
    perm, owner, routes, route_gates, dense, tokens, cotangent, mixed, token_grad, grads, *refs = refs
    side, full, picked, weights, pre, mult, own_acts, far_acts, table, *refs = refs
    data, recv, swap, relay, upper, order_ref, act_rows, grad_rows, gates, gate_col, both_col, *refs = refs
    load_sem, gate_sem, row_send, row_recv, fwd_send, fwd_recv, tok_send, tok_recv, *refs = refs
    act_sem, halve_send, halve_recv, swap_sem, out_sem, relay_send, relay_recv = refs

    row, col = lax.axis_index("dp"), lax.axis_index("expert")
    me = row * n_ex + col
    core, spot_x = row % 2, row // 2
    n_x = n_dp // 2
    chip = spot_x * n_ex + col
    block_units, feat = side.shape[1:]
    pick, share = picked.shape[2], upper.shape[0]
    slabs = n_ex // 2
    slab_units = share * n_dp
    padded = weights.shape[1] // (2 * n_dp)
    half_units = n_dp * padded
    width = full.shape[2]
    tok = tokens.shape[0]
    quarter = tok // n_dp
    half = full.shape[1] // 2
    dp_bits, ex_bits = log2(n_dp), log2(n_ex)
    bits = dp_bits + ex_bits
    sibling = peer(flip(me, ex_bits), n_ex)
    mesh_id = pl.DeviceIdType.MESH

    def remote(src, dst, send_sem, recv_sem, device):
        return pltpu.make_async_remote_copy(
            src_ref=src,
            dst_ref=dst,
            send_sem=send_sem,
            recv_sem=recv_sem,
            device_id=device,
            device_id_type=mesh_id,
        )

    def wait(view, sem):
        pltpu.make_async_copy(view, view, sem).wait()

    def place(at, device):
        where = device // n_ex
        start = where % 2 * half + where // 2 * (n_ex * quarter) + device % n_ex * quarter
        return full.at[at, pl.ds(pl.multiple_of(start, quarter), quarter), :]

    for at, source in enumerate((tokens, cotangent)):
        pltpu.make_async_copy(
            source.at[pl.ds(pl.multiple_of(row * quarter, quarter), quarter), :],
            place(at, me),
            load_sem.at[at],
        ).start()
    pltpu.make_async_copy(dense, side, load_sem.at[2]).start()
    for e in range(n_ex):
        chosen = jnp.where(routes[...] == e, route_gates[...], 0.0)
        table[e] = jnp.sum(chosen, axis=0, keepdims=True)

    if padded > pick:
        for k in range(3):
            for slot in range(2 * n_dp):
                rows = pl.ds(slot * padded + pick, padded - pick)
                weights[k, rows, :] = jnp.zeros((padded - pick, width), BF16)

    barrier = pltpu.get_barrier_semaphore()
    for mask in range(1, n_dp * n_ex):
        pl.semaphore_signal(
            barrier, inc=1, device_id=peer(flip_mask(me, mask), n_ex), device_id_type=mesh_id
        )
    upper[...] = (
        lax.broadcasted_iota(jnp.int32, (share, share), 0)
        < lax.broadcasted_iota(jnp.int32, (share, share), 1)
    ).astype(BF16)

    ex_order = list(range(ex_bits - 1, -1, -1))
    dp_order = [ex_bits + bit for bit in range(dp_bits - 1, -1, -1)]
    tok_orders = [
        ex_order + dp_order,
        ex_order[:-1] + [dp_order[0], ex_order[-1]] + dp_order[1:],
    ]

    def send_tokens(step):
        for at in range(2):
            order = tok_orders[at]

            def one(choice, carry, at=at, order=order):
                device = me
                for bit, other in enumerate(order[:step]):
                    mine = me // (1 << other) % 2
                    device = device + (choice // (1 << bit) % 2 - mine) * (1 << other)
                remote(
                    place(at, device),
                    place(at, device),
                    tok_send.at[at, step],
                    tok_recv.at[at, step],
                    peer(flip(me, order[step]), n_ex),
                ).start()
                return carry

            lax.fori_loop(0, 1 << step, one, 0)

    def wait_tokens(step, sem):
        for at in range(2):
            wait(full.at[at, pl.ds(0, (1 << step) * quarter), :], sem.at[at, step])

    def ranks(mask):
        return jnp.dot(mask.astype(BF16), upper[...], preferred_element_type=F32)

    def slab_rows(e):
        owned = jnp.full((1, slab_units), owner[e], jnp.int32)
        line = jnp.zeros((1, slab_units), jnp.int32)
        for slab in range(n_ex):
            start = slab % slabs * slab_units
            units = perm[slab // slabs : slab // slabs + 1, start : start + slab_units]
            line = jnp.where(owned == slab, units, line)
        return jnp.concatenate(
            [line[:, g * share : (g + 1) * share] for g in range(n_dp)], axis=0
        )

    def pick_rows(mask):
        target = flip_mask(col, mask)
        local = slab_rows(target) - row * block_units
        inside = jnp.logical_and(local >= 0, local < block_units)
        spots = jnp.where(inside, ranks(inside), -1.0)
        values = (local + 1).astype(F32)
        hots = []
        for g in range(n_dp):
            hit = spots[g : g + 1, :] == lax.broadcasted_iota(
                jnp.int32, (padded, share), 0
            ).astype(F32)
            units = jnp.sum(jnp.where(hit, values[g : g + 1, :], 0.0), axis=1, keepdims=True)
            hots.append(
                (
                    units.astype(jnp.int32) - 1
                    == lax.broadcasted_iota(jnp.int32, (padded, block_units), 1)
                ).astype(BF16)
            )
        hot = jnp.concatenate(hots, axis=0)
        for k in range(3):
            rows = jnp.dot(hot, side[k], preferred_element_type=F32).astype(BF16)
            for g in range(n_dp):
                picked[mask * n_dp + g, k] = rows[g * padded : g * padded + pick, :]

    def spot_of(holder, g, source_col):
        start = pl.multiple_of((g % 2 * n_dp + holder) * padded, padded)
        return weights.at[
            :, pl.ds(start, pick), pl.ds(pl.multiple_of(source_col * feat, feat), feat)
        ]

    def send_rows(mask, turn):
        z_mask, slot = mask // 2, mask % 2 * n_dp + turn
        g = flip_mask(row, turn)
        source = picked.at[mask * n_dp + g]
        if mask == 0 and turn == 0:
            pltpu.make_async_copy(source, spot_of(row, row, col), row_recv.at[col]).start()
        elif z_mask and slot:
            remote(
                source,
                relay.at[z_mask - 1, slot - 1],
                row_send.at[0],
                relay_recv.at[z_mask - 1, slot - 1],
                {"dp": row, "expert": flip_mask(col, 2 * z_mask)},
            ).start()
        else:
            remote(
                source,
                spot_of(row, g, col),
                row_send.at[0],
                row_recv.at[col],
                {"dp": g, "expert": flip_mask(col, mask)},
            ).start()

    def pass_rows(mask, turn):
        z_mask, slot = mask // 2, mask % 2 * n_dp + turn
        source = relay.at[z_mask - 1, slot - 1]
        source_col = flip_mask(col, 2 * z_mask)
        g = flip_mask(row, turn)
        wait(source, relay_recv.at[z_mask - 1, slot - 1])
        remote(
            source,
            spot_of(row, g, source_col),
            relay_send.at[0],
            row_recv.at[source_col],
            {"dp": g, "expert": flip_mask(col, mask % 2)},
        ).start()

    def step_tokens(step):
        wait_tokens(step - 1, tok_recv)
        send_tokens(step)

    def place_units():
        rows = slab_rows(col)
        mine = rows[:1]
        for g in range(1, n_dp):
            mine = jnp.where(row == g, rows[g : g + 1], mine)
        at_row = jnp.zeros((1, share), F32)
        for b in range(n_dp):
            inside = jnp.logical_and(mine >= b * block_units, mine < (b + 1) * block_units)
            at_row = at_row + jnp.where(inside, ranks(inside) + float(b * padded), 0.0)
        diagonal = lax.broadcasted_iota(jnp.int32, (share, share), 0) == lax.broadcasted_iota(
            jnp.int32, (share, share), 1
        )
        at_col = jnp.sum(jnp.where(diagonal, at_row, 0.0), axis=1, keepdims=True)
        order_ref[...] = (
            at_col.astype(jnp.int32) == lax.broadcasted_iota(jnp.int32, (share, half_units), 1)
        ).astype(BF16)

    def place_gates():
        wait(table.at[pl.ds(0, n_ex - 1)], gate_sem.at[0])
        wait(gates, gate_sem.at[1])
        copy_id = owner[col] // slabs
        lanes = lax.broadcasted_iota(jnp.int32, (quarter, tok), 1)
        below = lax.broadcasted_iota(jnp.int32, (quarter, tok), 0)
        for xq in range(n_x):

            def column(block, carry, xq=xq):
                hit = lanes == below + (xq * 2 + core) * quarter
                value = jnp.sum(jnp.where(hit, gates[block], 0.0), axis=1, keepdims=True)
                value = jnp.broadcast_to(value, (quarter, 128))
                blocks = jnp.full((quarter, 128), block * 2 // n_ex, jnp.int32)
                rows = pl.ds(pl.multiple_of((xq * n_ex + block) * quarter, quarter), quarter)
                gate_col[rows, :] = value
                both_col[rows, :] = value + (blocks == copy_id).astype(F32)
                return carry

            lax.fori_loop(0, n_ex, column, 0)

    my_rows = pl.ds(pl.multiple_of(core * half, half), half)
    my_units = pl.ds(pl.multiple_of(core * half_units, half_units), half_units)
    far_units = pl.ds(pl.multiple_of((1 - core) * half_units, half_units), half_units)
    n_tile = min(256, 2 * half_units)
    tiles = 2 * half_units // n_tile

    def columns(mask):
        return pl.ds(pl.multiple_of(flip_mask(col, mask) * feat, feat), feat)

    def forward(mask):
        f = flip_mask(col, mask)
        count = n_dp * pick
        wait(weights.at[:, pl.ds(0, count), columns(mask)], row_recv.at[f])
        for k in range(3):
            view = weights.at[k, my_units, columns(mask)]
            remote(view, view, fwd_send.at[0], fwd_recv.at[f], sibling).start()

    def accumulate(mask, first):
        for near in range(2):
            f = flip_mask(col, mask + near)
            wait(weights.at[:, far_units, columns(mask + near)], fwd_recv.at[f])
        both = pl.ds(pl.multiple_of(flip_mask(col, mask) // 2 * (2 * feat), 2 * feat), 2 * feat)

        def one(index, carry):
            k, n = index // tiles, index % tiles
            units = pl.ds(pl.multiple_of(n * n_tile, n_tile), n_tile)
            value = dot(full[k // 2, my_rows, both], weights[k, units, both], 1, 1)
            if first:
                pre[k, :, units] = value
            else:
                pre[k, :, units] = pre[k, :, units] + value
            return carry

        lax.fori_loop(0, 3 * tiles, one, 0)

    acts = {
        "pick": pick_rows,
        "send": send_rows,
        "pass": pass_rows,
        "tokens": step_tokens,
        "units": place_units,
        "gates": place_gates,
        "share": forward,
        "add": accumulate,
    }
    plan = gather_plan()
    wait(side, load_sem.at[2])
    pick_rows(*plan[0][1:])
    pl.semaphore_wait(barrier, n_dp * n_ex - 1)

    for at in range(2):
        wait(place(at, me), load_sem.at[at])
    send_tokens(0)
    pltpu.make_async_copy(table.at[col], gates.at[col], gate_sem.at[1]).start()
    for mask in range(1, n_ex):
        device = flip_mask(me, mask)
        remote(
            table.at[device % n_ex],
            gates.at[col],
            gate_sem.at[0],
            gate_sem.at[1],
            peer(device, n_ex),
        ).start()
    for name, *where in plan[1:]:
        acts[name](*where)

    r_tile = 32

    def activate(share_at, keep):
        units = pl.ds(pl.multiple_of(share_at * half_units, half_units), half_units)

        def one(index, carry):
            rows = pl.ds(pl.multiple_of(index * r_tile, r_tile), r_tile)
            reps = (1, half_units // 128)
            gate = jnp.tile(gate_col[rows, :], reps)
            both = jnp.tile(both_col[rows, :], reps)
            act, slope = silu_parts(pre[0, rows, units])
            up, d_hidden = pre[1, rows, units], pre[2, rows, units]
            values = (d_hidden * up * slope, d_hidden * act, act * up)
            for k, value in enumerate(values):
                mult[k, rows, units] = (both * value).astype(BF16)
                if keep:
                    own_acts[core, k, rows, :] = (gate * value).astype(BF16)
                else:
                    far_acts[k, rows, :] = (gate * value).astype(BF16)
            return carry

        lax.fori_loop(0, half // r_tile, one, 0)

    activate(1 - core, False)
    act_copy = remote(far_acts, own_acts.at[core], act_sem.at[0], act_sem.at[1], sibling)
    act_copy.start()
    activate(core, True)

    chip_bits = bits - 1
    x_place, y_place, z_low = chip_bits - 1, 0, 1
    rest = list(range(2, chip_bits - 1))
    classes = {
        "a": [x_place, y_place, z_low] + rest,
        "b": [y_place, z_low, x_place] + rest,
        "c": [z_low, x_place, y_place] + rest,
    }
    kinds = ["a", "a", "a", "c", "b", "b", "b", "c"]
    turns = [0, 4, 3, 1, 5, 7, 2, 6]
    chunk = data.shape[3]
    per_array = width // n_x // chunk
    r_rows = data.shape[2]

    def chip_peer(place_at):
        if place_at == x_place:
            return peer(flip(me, bits - 1), n_ex)
        return peer(flip(me, place_at), n_ex)

    def block_of(stream, step, choice, sent):
        order = classes[kinds[stream]]
        index = 0
        for place_at in order[: step + 1]:
            index = index + chip // (1 << place_at) % 2 * (1 << place_at)
        if sent:
            index = flip(index, order[step])
        for bit, place_at in enumerate(sorted(order[step + 1 :])):
            index = index + choice // (1 << bit) % 2 * (1 << place_at)
        return index

    def count(step):
        return 1 << (chip_bits - 1 - step)

    def offset(step):
        return (1 << chip_bits) - (1 << (chip_bits - step))

    def send(stream, step, choice):
        remote(
            data.at[stream, block_of(stream, step, choice, True)],
            recv.at[stream, offset(step) + choice],
            halve_send.at[stream, step],
            halve_recv.at[stream, step],
            chip_peer(classes[kinds[stream]][step]),
        ).start()

    def region(stream, step):
        return recv.at[stream, pl.ds(offset(step), count(step))]

    def number(stream, step, choice, sent):
        order = classes[kinds[stream]]
        later = sorted(order[step + 1 :])
        place_at = order[step + 1]
        mine_bit = chip // (1 << place_at) % 2
        value = (1 - mine_bit if sent else mine_bit) * (1 << later.index(place_at))
        for bit, other in enumerate(sorted(order[step + 2 :])):
            value = value + choice // (1 << bit) % 2 * (1 << later.index(other))
        return value

    def product(stream, xq):
        array, j = stream // per_array, stream % per_array
        cols = pl.ds(pl.multiple_of(xq * (width // n_x) + j * chunk, chunk), chunk)
        if array == 0:
            value = jnp.dot(mult[2], weights[2, :, cols], preferred_element_type=F32)
        else:
            value = jnp.dot(mult[0], weights[0, :, cols], preferred_element_type=F32)
            value = value + jnp.dot(mult[1], weights[1, :, cols], preferred_element_type=F32)
        value = value.astype(BF16).reshape(n_x, n_ex, quarter, chunk)
        for part in range(n_x):
            data[
                stream,
                pl.ds(pl.multiple_of(xq * n_ex, n_ex), n_ex),
                part * quarter : (part + 1) * quarter,
                :,
            ] = value[part]

    def begin(stream):
        def first(choice, carry):
            send(stream, 0, choice)
            return carry

        lax.fori_loop(0, count(0), first, 0)

    for stream in turns:
        if kinds[stream] == "a":
            product(stream, 1 - spot_x)
            begin(stream)
        else:

            def both_sides(side_at, carry, stream=stream):
                product(stream, side_at)
                return carry

            lax.fori_loop(0, n_x, both_sides, 0)
            begin(stream)
    for stream in turns:
        if kinds[stream] == "a":
            product(stream, spot_x)

    def weight_grad(k):
        for part in range(2):
            act_rows[:, part * half : (part + 1) * half] = dot(
                order_ref[...], own_acts[part, k], 1, 1
            ).astype(BF16)
        piece = min(512, width)

        def one(step, carry):
            where = pl.ds(pl.multiple_of(step * piece, piece), piece)
            grad_rows[k, :, where] = jnp.dot(
                act_rows[...], full[k // 2, :, where], preferred_element_type=F32
            ).astype(BF16)
            return carry

        lax.fori_loop(0, width // piece, one, 0)
        pltpu.make_async_copy(grad_rows.at[k], grads.at[0, k], out_sem.at[k]).start()

    def combine(stream, step):
        wait(region(stream, step), halve_recv.at[stream, step])
        for sent in (True, False):

            def add(choice, carry, sent=sent):
                block = block_of(stream, step + 1, choice, sent)
                slot = offset(step) + number(stream, step, choice, sent)
                total = data[stream, block].astype(F32) + recv[stream, slot].astype(F32)
                data[stream, block] = total.astype(BF16)
                if sent:
                    send(stream, step + 1, choice)
                return carry

            lax.fori_loop(0, count(step + 1), add, 0)

    wait_tokens(bits - 1, tok_recv)
    act_copy.wait()
    fill = {(0, 0): 0, (0, 3): 1, (0, 6): 2}
    for step in range(chip_bits - 1):
        for at, stream in enumerate(turns):
            if (step, at) in fill:
                weight_grad(fill[step, at])
            combine(stream, step)

    last = chip_bits - 1
    results = (mixed, token_grad)

    def finish(array, i, keep):
        owner_core = core if keep else 1 - core
        stream = array * per_array + owner_core * (per_array // 2) + i
        wait(recv.at[stream, pl.ds(offset(last), 1)], halve_recv.at[stream, last])
        total = (
            data[stream, chip].astype(F32) + recv[stream, offset(last)].astype(F32)
        ).astype(BF16)
        if keep:
            put(array, i, core, total)
        else:
            data[stream, chip] = total
            remote(
                data.at[stream, chip],
                swap.at[array, i],
                swap_sem.at[0],
                swap_sem.at[1],
                sibling,
            ).start()

    def put(array, i, which, total):
        for part in range(n_x):
            start = pl.multiple_of((part * 2 + which) * quarter, quarter)
            results[array][pl.ds(start, quarter), i * chunk : (i + 1) * chunk] = total[
                part * quarter : (part + 1) * quarter
            ]

    for keep in (False, True):
        for array in range(2):
            for i in range(per_array // 2):
                finish(array, i, keep)
    wait(swap, swap_sem.at[1])
    for array in range(2):
        for i in range(per_array // 2):
            put(array, i, 1 - core, swap[array, i])

    for k in range(3):
        pltpu.make_async_copy(grad_rows.at[k], grads.at[0, k], out_sem.at[k]).wait()
    wait(picked.at[pl.ds(0, n_dp * n_ex - 1)], row_send.at[0])
    wait(relay, relay_send.at[0])
    wait(weights.at[:, my_units, :], fwd_send.at[0])
    for step in range(bits):
        wait_tokens(step, tok_send)
    for step in range(chip_bits):
        for stream in range(len(kinds)):
            wait(region(stream, step), halve_send.at[stream, step])
    wait(swap, swap_sem.at[0])


def fused_step(
    n_dp, n_ex, unit_perm, slab_owner, routes, route_gates, dense_weights, tokens, cotangent
):
    _, block_units, feat = dense_weights.shape
    tok, width = tokens.shape
    share = unit_perm.shape[1] // (n_ex // 2) // n_dp
    pick = share // n_dp
    padded = -(-pick // 16) * 16
    half_units, half = n_dp * padded, n_ex * tok // 2
    blocks, bits, n_x = n_dp * n_ex, log2(n_dp * n_ex), n_dp // 2
    chips, chunk = blocks // 2, 256
    streams = 2 * (width // n_x // chunk)
    any_spec, vmem_spec = pl.BlockSpec(memory_space=pl.ANY), pl.BlockSpec(memory_space=pltpu.VMEM)
    r_rows = tok // 2
    results = pl.pallas_call(
        functools.partial(fused_kernel, n_dp, n_ex),
        out_shape=[
            jax.ShapeDtypeStruct((tok, width // n_dp), BF16),
            jax.ShapeDtypeStruct((tok, width // n_dp), BF16),
            jax.ShapeDtypeStruct((1, 3, share, width), BF16),
        ],
        in_specs=[
            vmem_spec,
            pl.BlockSpec(memory_space=pltpu.SMEM),
            vmem_spec,
            vmem_spec,
            any_spec,
            any_spec,
            any_spec,
        ],
        out_specs=[vmem_spec, vmem_spec, any_spec],
        scratch_shapes=[
            pltpu.VMEM((3, block_units, feat), BF16),
            pltpu.VMEM((2, n_ex * tok, width), BF16),
            pltpu.VMEM((blocks, 3, pick, feat), BF16),
            pltpu.VMEM((3, 2 * half_units, width), BF16),
            pltpu.VMEM((3, half, 2 * half_units), F32),
            pltpu.VMEM((3, half, 2 * half_units), BF16),
            pltpu.VMEM((2, 3, half, half_units), BF16),
            pltpu.VMEM((3, half, half_units), BF16),
            pltpu.VMEM((n_ex, 1, tok), F32),
            pltpu.VMEM((streams, chips, r_rows, chunk), BF16),
            pltpu.VMEM((streams, chips - 1, r_rows, chunk), BF16),
            pltpu.VMEM((2, streams // 4, r_rows, chunk), BF16),
            pltpu.VMEM((n_ex // 2 - 1, 2 * n_dp - 1, 3, pick, feat), BF16),
            pltpu.VMEM((share, share), BF16),
            pltpu.VMEM((share, half_units), BF16),
            pltpu.VMEM((share, n_ex * tok), BF16),
            pltpu.VMEM((3, share, width), BF16),
            pltpu.VMEM((n_ex, 1, tok), F32),
            pltpu.VMEM((half, 128), F32),
            pltpu.VMEM((half, 128), F32),
            pltpu.SemaphoreType.DMA((3,)),
            pltpu.SemaphoreType.DMA((2,)),
            pltpu.SemaphoreType.DMA((1,)),
            pltpu.SemaphoreType.DMA((n_ex,)),
            pltpu.SemaphoreType.DMA((1,)),
            pltpu.SemaphoreType.DMA((n_ex,)),
            pltpu.SemaphoreType.DMA((2, bits)),
            pltpu.SemaphoreType.DMA((2, bits)),
            pltpu.SemaphoreType.DMA((2,)),
            pltpu.SemaphoreType.DMA((streams, bits - 1)),
            pltpu.SemaphoreType.DMA((streams, bits - 1)),
            pltpu.SemaphoreType.DMA((2,)),
            pltpu.SemaphoreType.DMA((3,)),
            pltpu.SemaphoreType.DMA((1,)),
            pltpu.SemaphoreType.DMA((n_ex // 2 - 1, 2 * n_dp - 1)),
        ],
        compiler_params=pltpu.CompilerParams(
            collective_id=2, has_side_effects=True, vmem_limit_bytes=63 << 20
        ),
        name="fused_step",
    )(unit_perm, slab_owner, routes.T, route_gates.T, dense_weights, tokens, cotangent)
    pieces = len(publish_rows(share))
    return pl.pallas_call(
        publish_kernel,
        out_shape=[jax.ShapeDtypeStruct(result.shape, result.dtype) for result in results],
        in_specs=[any_spec] * 3,
        out_specs=[any_spec] * 3,
        scratch_shapes=[
            pltpu.VMEM((2, tok, width // n_dp), BF16),
            pltpu.VMEM((3, share, width), BF16),
            pltpu.SemaphoreType.DMA((2, 3 * pieces + 2)),
        ],
        compiler_params=pltpu.CompilerParams(vmem_limit_bytes=63 << 20),
        name="publish",
    )(*results)


def publish_rows(rows):
    size = -(-rows // 64) * 16
    return [(start, min(size, rows - start)) for start in range(0, rows, size)]


def publish_kernel(mixed, token_grad, grads, mixed_out, token_grad_out, grads_out, small, large, sem):
    moves = [
        (mixed, small.at[0], mixed_out),
        (token_grad, small.at[1], token_grad_out),
    ]
    for k in range(3):
        for start, size in publish_rows(large.shape[1]):
            rows = pl.ds(start, size)
            moves.append((grads.at[0, k, rows], large.at[k, rows], grads_out.at[0, k, rows]))
    for at, (source, middle, _) in enumerate(moves):
        pltpu.make_async_copy(source, middle, sem.at[0, at]).start()
    for at, (source, middle, target) in enumerate(moves):
        pltpu.make_async_copy(source, middle, sem.at[0, at]).wait()
        pltpu.make_async_copy(middle, target, sem.at[1, at]).start()
    for at, (_, middle, target) in enumerate(moves):
        pltpu.make_async_copy(middle, target, sem.at[1, at]).wait()


def gather_plain(n_dp, n_ex, row, picked, tokens, cotangent, table):
    _, pick, wide = picked.shape
    tok, width = tokens.shape
    arrived = lax.all_to_all(picked, ("dp", "expert"), split_axis=0, concat_axis=0, tiled=True)
    arrived = arrived.reshape(n_dp, n_ex, pick, 3, wide // 3)
    weights = jnp.transpose(arrived, (3, 0, 2, 1, 4)).reshape(3, n_dp * pick, width)
    part = width // n_dp
    both = jnp.concatenate(
        [
            lax.dynamic_slice(tokens, (0, row * part), (tok, part)),
            lax.dynamic_slice(cotangent, (0, row * part), (tok, part)),
        ],
        axis=1,
    )
    both = lax.all_gather(both, "expert", axis=0, tiled=True)
    both = lax.all_gather(both, "dp", axis=0, tiled=False)
    all_x = jnp.transpose(both[:, :, :part], (1, 0, 2)).reshape(n_ex * tok, width)
    all_c = jnp.transpose(both[:, :, part:], (1, 0, 2)).reshape(n_ex * tok, width)
    gates = lax.all_to_all(table, "expert", split_axis=0, concat_axis=0, tiled=True)
    return weights, all_x, all_c, gates


def body(dense_weights, tokens, cotangent, routes, route_gates, unit_perm, slab_owner):
    n_dp = lax.axis_size("dp")
    n_ex = lax.axis_size("expert")
    row = lax.axis_index("dp")
    col = lax.axis_index("expert")
    _, block_units, feat = dense_weights.shape
    copies, total_units = unit_perm.shape
    slabs = n_ex // copies
    slab_units = total_units // slabs
    share = slab_units // n_dp
    pick = share // n_dp
    tok, width = tokens.shape

    shares = unit_perm.reshape(n_ex, n_dp, share)
    padded = -(-pick // 16) * 16
    if (
        copies == 2
        and slab_units % 128 == 0
        and pick % 8 == 0
        and feat % 256 == 0
        and n_dp * padded % 128 == 0
        and 2 * n_dp * padded % 256 == 0
        and n_dp == 4
        and n_ex == 8
        and width == n_dp * 512
        and tok == 128
    ):
        return tuple(
            fused_step(
                n_dp,
                n_ex,
                unit_perm,
                slab_owner,
                routes,
                route_gates,
                dense_weights,
                tokens,
                cotangent,
            )
        )
    gate_table = jnp.sum(
        jnp.where(
            routes[None, :, :] == lax.broadcasted_iota(jnp.int32, (n_ex, 1, 1), 0),
            route_gates[None, :, :],
            0.0,
        ),
        axis=2,
    )
    dest = jnp.transpose(shares[slab_owner], (1, 0, 2)).reshape(n_dp * n_ex, share)
    mask, rank = block_ranks(dest // block_units, row)
    place = jnp.where(mask, rank, -1)
    hit = place[:, None, :] == lax.broadcasted_iota(jnp.int32, (1, pick, 1), 1)
    units = jnp.sum(jnp.where(hit, (dest - row * block_units)[:, None, :], 0), axis=2)
    onehot = (
        units.reshape(-1, 1) == lax.broadcasted_iota(jnp.int32, (1, block_units), 1)
    ).astype(BF16)
    side = jnp.concatenate([dense_weights[0], dense_weights[1], dense_weights[2]], axis=1)
    picked = dot(onehot, side, 1, 0).astype(BF16)
    picked = picked.reshape(n_dp * n_ex, pick, 3 * feat)
    mine = lax.dynamic_slice(
        shares, (slab_owner[col], row, 0), (1, 1, share)
    ).reshape(1, share)
    mine_block = mine // block_units
    mask, rank = block_ranks(
        jnp.broadcast_to(mine_block, (n_dp, share)),
        lax.broadcasted_iota(jnp.int32, (n_dp, 1), 0),
    )
    at = jnp.sum(
        jnp.where(mask, rank + lax.broadcasted_iota(jnp.int32, (n_dp, 1), 0) * pick, 0), axis=0
    )
    order = (lax.broadcasted_iota(jnp.int32, (share, share), 1) == at[:, None]).astype(BF16)

    weights, all_x, all_c, gate = gather_plain(
        n_dp, n_ex, row, picked, tokens, cotangent, gate_table
    )
    w_gate, w_up, w_down = weights[0], weights[1], weights[2]
    gate = gate.reshape(n_ex * tok, 1)
    copy_id = slab_owner[col] // slabs
    owner_block = lax.broadcasted_iota(jnp.int32, (n_ex, tok), 0).reshape(n_ex * tok, 1)
    both_weight = gate + (owner_block * copies // n_ex == copy_id).astype(F32)

    pre_gate = dot(all_x, w_gate, 1, 1)
    pre_up = dot(all_x, w_up, 1, 1)
    d_hidden = dot(all_c, w_down, 1, 1)
    act, slope = silu_parts(pre_gate)
    hidden = act * pre_up
    d_gate = d_hidden * pre_up * slope
    d_up = d_hidden * act

    out = dot((both_weight * hidden).astype(BF16), w_down, 1, 0).astype(BF16)
    back = (
        dot((both_weight * d_gate).astype(BF16), w_gate, 1, 0)
        + dot((both_weight * d_up).astype(BF16), w_up, 1, 0)
    ).astype(BF16)

    acts = [(gate * values).astype(BF16) for values in (d_gate, d_up, hidden)]
    if out.size * out.dtype.itemsize <= 1 << 23:
        mixed, token_grad, weight_grads = halving_sum(
            n_dp, n_ex, [out, back], acts + [order], [all_x, all_c]
        )
    else:
        acts = [dot(order, values, 1, 1).astype(BF16) for values in acts]
        weight_grads = jnp.stack(
            [dot(acts[0], all_x, 1, 0), dot(acts[1], all_x, 1, 0), dot(acts[2], all_c, 1, 0)]
        ).astype(BF16)[None]
        (mixed,) = halving_sum(n_dp, n_ex, [out])
        (token_grad,) = halving_sum(n_dp, n_ex, [back])
    return (mixed, token_grad, weight_grads)


def solution(mesh):
    in_specs = (
        P(None, "dp", "expert"),
        P("expert", None),
        P("expert", None),
        P("expert", None),
        P("expert", None),
        P(),
        P(),
    )
    out_specs = (P("expert", "dp"), P("expert", "dp"), P("expert", None, "dp", None))
    return jax.shard_map(body, mesh=mesh, in_specs=in_specs, out_specs=out_specs, check_vma=False)
```

```python
import functools

import jax
import jax.numpy as jnp
from jax import lax
from jax.experimental import pallas as pl
from jax.experimental.pallas import tpu as pltpu
from jax.sharding import PartitionSpec as P

F32 = jnp.float32
BF16 = jnp.bfloat16


def silu_parts(preact):
    sigmoid_value = jax.nn.sigmoid(preact)
    return (preact * sigmoid_value, sigmoid_value * (1.0 + preact * (1.0 - sigmoid_value)))


def dot(left, right, left_dim, right_dim):
    return lax.dot_general(
        left, right, (((left_dim,), (right_dim,)), ((), ())), preferred_element_type=F32
    )


def block_ranks(blocks, block):
    width = blocks.shape[-1]
    mask = blocks == block
    upper = lax.broadcasted_iota(jnp.int32, (width, width), 0) < lax.broadcasted_iota(
        jnp.int32, (width, width), 1
    )
    rank = jnp.dot(mask.astype(BF16), upper.astype(BF16), preferred_element_type=F32)
    return mask, rank.astype(jnp.int32)


def log2(count):
    return count.bit_length() - 1


def flip(index, place):
    return index + (1 - 2 * (index // (1 << place) % 2)) * (1 << place)


def peer(device, n_ex):
    return {"dp": device // n_ex, "expert": device % n_ex}


STREAMS = 4


def halving_orders(dp_bits, ex_bits):
    rest = [ex_bits + bit for bit in range(1, dp_bits)] + list(range(ex_bits))
    turns = [[0, 1, 2], [1, 2, 0], [2, 0, 1], [1, 0, 2]]
    orders = []
    for turn in turns:
        head = [rest[at] for at in turn if at < len(rest)]
        orders.append([ex_bits] + head + rest[len(head) :])
    return orders


def halving_kernel(n_dp, n_ex, n_arrays, with_grads, *refs):
    ins, refs = refs[:n_arrays], refs[n_arrays:]
    acts, order_ref, fulls, refs = (
        (refs[:3], refs[3], refs[4:6], refs[6:]) if with_grads else ((), None, (), refs)
    )
    outs, refs = refs[:n_arrays], refs[n_arrays:]
    if with_grads:
        grads, full_rows, grad_rows, act_rows, full_sem, grad_sem = refs[0], *refs[-5:]
        refs = refs[1:-5]
    data, recv, load_sem, send_sem, recv_sem = refs
    me = lax.axis_index("dp") * n_ex + lax.axis_index("expert")
    bits = log2(n_dp) + log2(n_ex)
    orders = halving_orders(log2(n_dp), log2(n_ex))
    rows, part = data.shape[2:]
    splits = STREAMS // n_arrays

    for stream in range(STREAMS):
        source, at = ins[stream // splits], stream % splits
        for g in range(n_dp):

            def load(e, carry, source=source, at=at, g=g, stream=stream):
                start = pl.multiple_of(e * (rows * splits) + at * rows, rows)
                pltpu.make_async_copy(
                    source.at[pl.ds(start, rows), pl.ds(g * part, part)],
                    data.at[stream, g * n_ex + e],
                    load_sem.at[stream],
                ).start()
                return carry

            lax.fori_loop(0, n_ex, load, 0)

    for at, full in enumerate(fulls):
        pltpu.make_async_copy(full, full_rows.at[at], full_sem.at[at]).start()

    def weight_grad(k):
        if k != 1:
            at = k // 2
            pltpu.make_async_copy(fulls[at], full_rows.at[at], full_sem.at[at]).wait()
        width = full_rows.shape[-1]
        piece = min(512, width)
        act_rows[...] = dot(order_ref[...], acts[k][...], 1, 1).astype(BF16)

        def product(step, carry):
            lanes = pl.ds(pl.multiple_of(step * piece, piece), piece)
            grad_rows[k, :, lanes] = jnp.dot(
                act_rows[...], full_rows[k // 2, :, lanes], preferred_element_type=F32
            ).astype(BF16)
            return carry

        lax.fori_loop(0, width // piece, product, 0)
        pltpu.make_async_copy(grad_rows.at[k], grads.at[0, k], grad_sem.at[k]).start()

    barrier = pltpu.get_barrier_semaphore()
    for place in range(bits):
        pl.semaphore_signal(
            barrier,
            inc=1,
            device_id=peer(flip(me, place), n_ex),
            device_id_type=pl.DeviceIdType.MESH,
        )
    pl.semaphore_wait(barrier, bits)

    def block_of(stream, step, choice, sent):
        order = orders[stream]
        index = 0
        for place in order[: step + 1]:
            index = index + me // (1 << place) % 2 * (1 << place)
        if sent:
            index = flip(index, order[step])
        for bit, place in enumerate(sorted(order[step + 1 :])):
            index = index + choice // (1 << bit) % 2 * (1 << place)
        return index

    def count(step):
        return 1 << (bits - 1 - step)

    def offset(step):
        return (1 << bits) - (1 << (bits - step))

    def send(stream, step, choice):
        pltpu.make_async_remote_copy(
            src_ref=data.at[stream, block_of(stream, step, choice, True)],
            dst_ref=recv.at[stream, offset(step) + choice],
            send_sem=send_sem.at[stream, step],
            recv_sem=recv_sem.at[stream, step],
            device_id=peer(flip(me, orders[stream][step]), n_ex),
            device_id_type=pl.DeviceIdType.MESH,
        ).start()

    def region(stream, step):
        view = recv.at[stream, pl.ds(offset(step), count(step))]
        return pltpu.make_async_remote_copy(
            src_ref=view,
            dst_ref=view,
            send_sem=send_sem.at[stream, step],
            recv_sem=recv_sem.at[stream, step],
            device_id=peer(flip(me, orders[stream][step]), n_ex),
            device_id_type=pl.DeviceIdType.MESH,
        )

    def number(stream, step, choice, sent):
        order = orders[stream]
        later = sorted(order[step + 1 :])
        place = order[step + 1]
        mine = me // (1 << place) % 2
        value = (1 - mine if sent else mine) * (1 << later.index(place))
        for bit, other in enumerate(sorted(order[step + 2 :])):
            value = value + choice // (1 << bit) % 2 * (1 << later.index(other))
        return value

    for stream in range(STREAMS):
        pltpu.make_async_copy(data.at[stream], data.at[stream], load_sem.at[stream]).wait()

        def first(choice, carry, stream=stream):
            send(stream, 0, choice)
            return carry

        lax.fori_loop(0, count(0), first, 0)

    if with_grads:
        weight_grad(0)
    for step in range(bits):
        for stream in range(STREAMS):
            region(stream, step).wait_recv()
            if step == bits - 1:
                total = data[stream, me].astype(F32) + recv[stream, offset(step)].astype(F32)
                outs[stream // splits][pl.ds(stream % splits * rows, rows), :] = total.astype(BF16)
                continue
            for sent in (True, False):

                def add(choice, carry, stream=stream, step=step, sent=sent):
                    block = block_of(stream, step + 1, choice, sent)
                    slot = offset(step) + number(stream, step, choice, sent)
                    total = data[stream, block].astype(F32) + recv[stream, slot].astype(F32)
                    data[stream, block] = total.astype(BF16)
                    if sent:
                        send(stream, step + 1, choice)
                    return carry

                lax.fori_loop(0, count(step + 1), add, 0)
        if step < 2 and with_grads:
            weight_grad(step + 1)

    if with_grads:
        for k in range(3):
            pltpu.make_async_copy(grad_rows.at[k], grads.at[0, k], grad_sem.at[k]).wait()
    for step in range(bits):
        for stream in range(STREAMS):
            region(stream, step).wait_send()


def halving_sum(n_dp, n_ex, arrays, acts=(), fulls=()):
    total, width = arrays[0].shape
    tok, part, n_arrays = total // n_ex, width // n_dp, len(arrays)
    rows = tok * n_arrays // STREAMS
    blocks = n_dp * n_ex
    steps = log2(blocks)
    any_spec, vmem_spec = pl.BlockSpec(memory_space=pl.ANY), pl.BlockSpec(memory_space=pltpu.VMEM)
    out_shape = [jax.ShapeDtypeStruct((tok, part), BF16)] * n_arrays
    out_specs = [vmem_spec] * n_arrays
    scratch = [
        pltpu.VMEM((STREAMS, blocks, rows, part), BF16),
        pltpu.VMEM((STREAMS, blocks - 1, rows, part), BF16),
        pltpu.SemaphoreType.DMA((STREAMS,)),
        pltpu.SemaphoreType.DMA((STREAMS, steps)),
        pltpu.SemaphoreType.DMA((STREAMS, steps)),
    ]
    if acts:
        share = acts[0].shape[1]
        out_shape = out_shape + [jax.ShapeDtypeStruct((1, 3, share, width), BF16)]
        out_specs = out_specs + [any_spec]
        scratch = scratch + [
            pltpu.VMEM((2, total, width), BF16),
            pltpu.VMEM((3, share, width), BF16),
            pltpu.VMEM((share, total), BF16),
            pltpu.SemaphoreType.DMA((2,)),
            pltpu.SemaphoreType.DMA((3,)),
        ]
    return pl.pallas_call(
        functools.partial(halving_kernel, n_dp, n_ex, n_arrays, bool(acts)),
        out_shape=out_shape,
        in_specs=[any_spec] * n_arrays + [vmem_spec] * len(acts) + [any_spec] * len(fulls),
        out_specs=out_specs,
        scratch_shapes=scratch,
        compiler_params=pltpu.CompilerParams(
            collective_id=1, has_side_effects=True, vmem_limit_bytes=60 << 20
        ),
        name="halving_sum",
    )(*arrays, *acts, *fulls)


def flip_mask(index, mask):
    place = 0
    while mask >> place:
        if mask >> place & 1:
            index = flip(index, place)
        place += 1
    return index


def gather_plan():
    every = (3, 2, 1, 0)

    def pick(*masks):
        return [("pick", mask) for mask in masks]

    def send(mask, *turns):
        return [("send", mask, turn) for turn in turns]

    def relay(mask, *turns):
        return [("pass", mask, turn) for turn in turns]

    def shared(*masks):
        return [("share", mask) for mask in masks]

    plan = pick(5) + send(5, 3, 2) + pick(1) + send(1, *every) + pick(0) + send(0, *every)
    plan += send(5, 1, 0) + [("units",), ("tokens", 1)]
    plan += pick(4) + send(4, 3, 2, 1) + pick(3) + send(3, *every) + relay(5, 3, 2)
    plan += [("gates",), ("tokens", 2)]
    plan += pick(7) + send(7, 3, 2) + pick(2) + send(2, *every) + relay(5, 1, 0)
    plan += [("tokens", 3)]
    plan += relay(3, *every) + pick(6) + send(4, 0) + send(6, 3, 2) + send(7, 1)
    plan += send(6, 1) + send(7, 0) + send(6, 0)
    plan += relay(4, 3, 2, 1) + relay(2, 3, 2, 1) + relay(7, 3, 2)
    plan += [("tokens", 4)]
    plan += shared(1, 0, 3, 2) + [("add", 0, True)] + relay(6, 3, 2)
    plan += shared(5, 4) + [("add", 2, False)] + relay(7, 1) + relay(6, 1) + relay(7, 0)
    plan += [("add", 4, False)] + shared(7, 6) + [("add", 6, False)]
    return plan


def fused_kernel(n_dp, n_ex, *refs):
    perm, owner, routes, route_gates, dense, tokens, cotangent, mixed, token_grad, grads, *refs = refs
    side, full, picked, weights, pre, mult, own_acts, far_acts, table, *refs = refs
    data, recv, swap, relay, upper, order_ref, act_rows, grad_rows, gates, gate_col, both_col, *refs = refs
    load_sem, gate_sem, row_send, row_recv, fwd_send, fwd_recv, tok_send, tok_recv, *refs = refs
    act_sem, halve_send, halve_recv, swap_sem, out_sem, relay_send, relay_recv = refs

    row, col = lax.axis_index("dp"), lax.axis_index("expert")
    me = row * n_ex + col
    core, spot_x = row % 2, row // 2
    n_x = n_dp // 2
    chip = spot_x * n_ex + col
    block_units, feat = side.shape[1:]
    pick, share = picked.shape[2], upper.shape[0]
    slabs = n_ex // 2
    slab_units = share * n_dp
    padded = weights.shape[1] // (2 * n_dp)
    half_units = n_dp * padded
    width = full.shape[2]
    tok = tokens.shape[0]
    quarter = tok // n_dp
    half = full.shape[1] // 2
    dp_bits, ex_bits = log2(n_dp), log2(n_ex)
    bits = dp_bits + ex_bits
    sibling = peer(flip(me, ex_bits), n_ex)
    mesh_id = pl.DeviceIdType.MESH

    def remote(src, dst, send_sem, recv_sem, device):
        return pltpu.make_async_remote_copy(
            src_ref=src,
            dst_ref=dst,
            send_sem=send_sem,
            recv_sem=recv_sem,
            device_id=device,
            device_id_type=mesh_id,
        )

    def wait(view, sem):
        pltpu.make_async_copy(view, view, sem).wait()

    def place(at, device):
        where = device // n_ex
        start = where % 2 * half + where // 2 * (n_ex * quarter) + device % n_ex * quarter
        return full.at[at, pl.ds(pl.multiple_of(start, quarter), quarter), :]

    for at, source in enumerate((tokens, cotangent)):
        pltpu.make_async_copy(
            source.at[pl.ds(pl.multiple_of(row * quarter, quarter), quarter), :],
            place(at, me),
            load_sem.at[at],
        ).start()
    pltpu.make_async_copy(dense, side, load_sem.at[2]).start()
    for e in range(n_ex):
        chosen = jnp.where(routes[...] == e, route_gates[...], 0.0)
        table[e] = jnp.sum(chosen, axis=0, keepdims=True)

    if padded > pick:
        for k in range(3):
            for slot in range(2 * n_dp):
                rows = pl.ds(slot * padded + pick, padded - pick)
                weights[k, rows, :] = jnp.zeros((padded - pick, width), BF16)

    barrier = pltpu.get_barrier_semaphore()
    for mask in range(1, n_dp * n_ex):
        pl.semaphore_signal(
            barrier, inc=1, device_id=peer(flip_mask(me, mask), n_ex), device_id_type=mesh_id
        )
    upper[...] = (
        lax.broadcasted_iota(jnp.int32, (share, share), 0)
        < lax.broadcasted_iota(jnp.int32, (share, share), 1)
    ).astype(BF16)

    ex_order = list(range(ex_bits - 1, -1, -1))
    dp_order = [ex_bits + bit for bit in range(dp_bits - 1, -1, -1)]
    tok_orders = [
        ex_order + dp_order,
        ex_order[:-1] + [dp_order[0], ex_order[-1]] + dp_order[1:],
    ]

    def send_tokens(step):
        for at in range(2):
            order = tok_orders[at]

            def one(choice, carry, at=at, order=order):
                device = me
                for bit, other in enumerate(order[:step]):
                    mine = me // (1 << other) % 2
                    device = device + (choice // (1 << bit) % 2 - mine) * (1 << other)
                remote(
                    place(at, device),
                    place(at, device),
                    tok_send.at[at, step],
                    tok_recv.at[at, step],
                    peer(flip(me, order[step]), n_ex),
                ).start()
                return carry

            lax.fori_loop(0, 1 << step, one, 0)

    def wait_tokens(step, sem):
        for at in range(2):
            wait(full.at[at, pl.ds(0, (1 << step) * quarter), :], sem.at[at, step])

    def ranks(mask):
        return jnp.dot(mask.astype(BF16), upper[...], preferred_element_type=F32)

    def slab_rows(e):
        owned = jnp.full((1, slab_units), owner[e], jnp.int32)
        line = jnp.zeros((1, slab_units), jnp.int32)
        for slab in range(n_ex):
            start = slab % slabs * slab_units
            units = perm[slab // slabs : slab // slabs + 1, start : start + slab_units]
            line = jnp.where(owned == slab, units, line)
        return jnp.concatenate(
            [line[:, g * share : (g + 1) * share] for g in range(n_dp)], axis=0
        )

    def pick_rows(mask):
        target = flip_mask(col, mask)
        local = slab_rows(target) - row * block_units
        inside = jnp.logical_and(local >= 0, local < block_units)
        spots = jnp.where(inside, ranks(inside), -1.0)
        values = (local + 1).astype(F32)
        hots = []
        for g in range(n_dp):
            hit = spots[g : g + 1, :] == lax.broadcasted_iota(
                jnp.int32, (padded, share), 0
            ).astype(F32)
            units = jnp.sum(jnp.where(hit, values[g : g + 1, :], 0.0), axis=1, keepdims=True)
            hots.append(
                (
                    units.astype(jnp.int32) - 1
                    == lax.broadcasted_iota(jnp.int32, (padded, block_units), 1)
                ).astype(BF16)
            )
        hot = jnp.concatenate(hots, axis=0)
        for k in range(3):
            rows = jnp.dot(hot, side[k], preferred_element_type=F32).astype(BF16)
            for g in range(n_dp):
                picked[mask * n_dp + g, k] = rows[g * padded : g * padded + pick, :]

    def spot_of(holder, g, source_col):
        start = pl.multiple_of((g % 2 * n_dp + holder) * padded, padded)
        return weights.at[
            :, pl.ds(start, pick), pl.ds(pl.multiple_of(source_col * feat, feat), feat)
        ]

    def send_rows(mask, turn):
        z_mask, slot = mask // 2, mask % 2 * n_dp + turn
        g = flip_mask(row, turn)
        source = picked.at[mask * n_dp + g]
        if mask == 0 and turn == 0:
            pltpu.make_async_copy(source, spot_of(row, row, col), row_recv.at[col]).start()
        elif z_mask and slot:
            remote(
                source,
                relay.at[z_mask - 1, slot - 1],
                row_send.at[0],
                relay_recv.at[z_mask - 1, slot - 1],
                {"dp": row, "expert": flip_mask(col, 2 * z_mask)},
            ).start()
        else:
            remote(
                source,
                spot_of(row, g, col),
                row_send.at[0],
                row_recv.at[col],
                {"dp": g, "expert": flip_mask(col, mask)},
            ).start()

    def pass_rows(mask, turn):
        z_mask, slot = mask // 2, mask % 2 * n_dp + turn
        source = relay.at[z_mask - 1, slot - 1]
        source_col = flip_mask(col, 2 * z_mask)
        g = flip_mask(row, turn)
        wait(source, relay_recv.at[z_mask - 1, slot - 1])
        remote(
            source,
            spot_of(row, g, source_col),
            relay_send.at[0],
            row_recv.at[source_col],
            {"dp": g, "expert": flip_mask(col, mask % 2)},
        ).start()

    def step_tokens(step):
        wait_tokens(step - 1, tok_recv)
        send_tokens(step)

    def place_units():
        rows = slab_rows(col)
        mine = rows[:1]
        for g in range(1, n_dp):
            mine = jnp.where(row == g, rows[g : g + 1], mine)
        at_row = jnp.zeros((1, share), F32)
        for b in range(n_dp):
            inside = jnp.logical_and(mine >= b * block_units, mine < (b + 1) * block_units)
            at_row = at_row + jnp.where(inside, ranks(inside) + float(b * padded), 0.0)
        diagonal = lax.broadcasted_iota(jnp.int32, (share, share), 0) == lax.broadcasted_iota(
            jnp.int32, (share, share), 1
        )
        at_col = jnp.sum(jnp.where(diagonal, at_row, 0.0), axis=1, keepdims=True)
        order_ref[...] = (
            at_col.astype(jnp.int32) == lax.broadcasted_iota(jnp.int32, (share, half_units), 1)
        ).astype(BF16)

    def place_gates():
        wait(table.at[pl.ds(0, n_ex - 1)], gate_sem.at[0])
        wait(gates, gate_sem.at[1])
        copy_id = owner[col] // slabs
        lanes = lax.broadcasted_iota(jnp.int32, (quarter, tok), 1)
        below = lax.broadcasted_iota(jnp.int32, (quarter, tok), 0)
        for xq in range(n_x):

            def column(block, carry, xq=xq):
                hit = lanes == below + (xq * 2 + core) * quarter
                value = jnp.sum(jnp.where(hit, gates[block], 0.0), axis=1, keepdims=True)
                value = jnp.broadcast_to(value, (quarter, 128))
                blocks = jnp.full((quarter, 128), block * 2 // n_ex, jnp.int32)
                rows = pl.ds(pl.multiple_of((xq * n_ex + block) * quarter, quarter), quarter)
                gate_col[rows, :] = value
                both_col[rows, :] = value + (blocks == copy_id).astype(F32)
                return carry

            lax.fori_loop(0, n_ex, column, 0)

    my_rows = pl.ds(pl.multiple_of(core * half, half), half)
    my_units = pl.ds(pl.multiple_of(core * half_units, half_units), half_units)
    far_units = pl.ds(pl.multiple_of((1 - core) * half_units, half_units), half_units)
    n_tile = min(256, 2 * half_units)
    tiles = 2 * half_units // n_tile

    def columns(mask):
        return pl.ds(pl.multiple_of(flip_mask(col, mask) * feat, feat), feat)

    def forward(mask):
        f = flip_mask(col, mask)
        count = n_dp * pick
        wait(weights.at[:, pl.ds(0, count), columns(mask)], row_recv.at[f])
        for k in range(3):
            view = weights.at[k, my_units, columns(mask)]
            remote(view, view, fwd_send.at[0], fwd_recv.at[f], sibling).start()

    def accumulate(mask, first):
        for near in range(2):
            f = flip_mask(col, mask + near)
            wait(weights.at[:, far_units, columns(mask + near)], fwd_recv.at[f])
        both = pl.ds(pl.multiple_of(flip_mask(col, mask) // 2 * (2 * feat), 2 * feat), 2 * feat)

        def one(index, carry):
            k, n = index // tiles, index % tiles
            units = pl.ds(pl.multiple_of(n * n_tile, n_tile), n_tile)
            value = dot(full[k // 2, my_rows, both], weights[k, units, both], 1, 1)
            if first:
                pre[k, :, units] = value
            else:
                pre[k, :, units] = pre[k, :, units] + value
            return carry

        lax.fori_loop(0, 3 * tiles, one, 0)

    acts = {
        "pick": pick_rows,
        "send": send_rows,
        "pass": pass_rows,
        "tokens": step_tokens,
        "units": place_units,
        "gates": place_gates,
        "share": forward,
        "add": accumulate,
    }
    plan = gather_plan()
    wait(side, load_sem.at[2])
    pick_rows(*plan[0][1:])
    pl.semaphore_wait(barrier, n_dp * n_ex - 1)

    for at in range(2):
        wait(place(at, me), load_sem.at[at])
    send_tokens(0)
    pltpu.make_async_copy(table.at[col], gates.at[col], gate_sem.at[1]).start()
    for mask in range(1, n_ex):
        device = flip_mask(me, mask)
        remote(
            table.at[device % n_ex],
            gates.at[col],
            gate_sem.at[0],
            gate_sem.at[1],
            peer(device, n_ex),
        ).start()
    for name, *where in plan[1:]:
        acts[name](*where)

    r_tile = 32

    def activate(share_at, keep):
        units = pl.ds(pl.multiple_of(share_at * half_units, half_units), half_units)

        def one(index, carry):
            rows = pl.ds(pl.multiple_of(index * r_tile, r_tile), r_tile)
            reps = (1, half_units // 128)
            gate = jnp.tile(gate_col[rows, :], reps)
            both = jnp.tile(both_col[rows, :], reps)
            act, slope = silu_parts(pre[0, rows, units])
            up, d_hidden = pre[1, rows, units], pre[2, rows, units]
            values = (d_hidden * up * slope, d_hidden * act, act * up)
            for k, value in enumerate(values):
                mult[k, rows, units] = (both * value).astype(BF16)
                if keep:
                    own_acts[core, k, rows, :] = (gate * value).astype(BF16)
                else:
                    far_acts[k, rows, :] = (gate * value).astype(BF16)
            return carry

        lax.fori_loop(0, half // r_tile, one, 0)

    activate(1 - core, False)
    act_copy = remote(far_acts, own_acts.at[core], act_sem.at[0], act_sem.at[1], sibling)
    act_copy.start()
    activate(core, True)

    chip_bits = bits - 1
    x_place, y_place, z_low = chip_bits - 1, 0, 1
    rest = list(range(2, chip_bits - 1))
    classes = {
        "a": [x_place, y_place, z_low] + rest,
        "b": [y_place, z_low, x_place] + rest,
        "c": [z_low, x_place, y_place] + rest,
    }
    kinds = ["a", "a", "a", "c", "b", "b", "b", "c"]
    turns = [0, 4, 3, 1, 5, 7, 2, 6]
    chunk = data.shape[3]
    per_array = width // n_x // chunk
    r_rows = data.shape[2]

    def chip_peer(place_at):
        if place_at == x_place:
            return peer(flip(me, bits - 1), n_ex)
        return peer(flip(me, place_at), n_ex)

    def block_of(stream, step, choice, sent):
        order = classes[kinds[stream]]
        index = 0
        for place_at in order[: step + 1]:
            index = index + chip // (1 << place_at) % 2 * (1 << place_at)
        if sent:
            index = flip(index, order[step])
        for bit, place_at in enumerate(sorted(order[step + 1 :])):
            index = index + choice // (1 << bit) % 2 * (1 << place_at)
        return index

    def count(step):
        return 1 << (chip_bits - 1 - step)

    def offset(step):
        return (1 << chip_bits) - (1 << (chip_bits - step))

    def send(stream, step, choice):
        remote(
            data.at[stream, block_of(stream, step, choice, True)],
            recv.at[stream, offset(step) + choice],
            halve_send.at[stream, step],
            halve_recv.at[stream, step],
            chip_peer(classes[kinds[stream]][step]),
        ).start()

    def region(stream, step):
        return recv.at[stream, pl.ds(offset(step), count(step))]

    def number(stream, step, choice, sent):
        order = classes[kinds[stream]]
        later = sorted(order[step + 1 :])
        place_at = order[step + 1]
        mine_bit = chip // (1 << place_at) % 2
        value = (1 - mine_bit if sent else mine_bit) * (1 << later.index(place_at))
        for bit, other in enumerate(sorted(order[step + 2 :])):
            value = value + choice // (1 << bit) % 2 * (1 << later.index(other))
        return value

    def product(stream, xq):
        array, j = stream // per_array, stream % per_array
        cols = pl.ds(pl.multiple_of(xq * (width // n_x) + j * chunk, chunk), chunk)
        if array == 0:
            value = jnp.dot(mult[2], weights[2, :, cols], preferred_element_type=F32)
        else:
            value = jnp.dot(mult[0], weights[0, :, cols], preferred_element_type=F32)
            value = value + jnp.dot(mult[1], weights[1, :, cols], preferred_element_type=F32)
        value = value.astype(BF16).reshape(n_x, n_ex, quarter, chunk)
        for part in range(n_x):
            data[
                stream,
                pl.ds(pl.multiple_of(xq * n_ex, n_ex), n_ex),
                part * quarter : (part + 1) * quarter,
                :,
            ] = value[part]

    def begin(stream):
        def first(choice, carry):
            send(stream, 0, choice)
            return carry

        lax.fori_loop(0, count(0), first, 0)

    for stream in turns:
        if kinds[stream] == "a":
            product(stream, 1 - spot_x)
            begin(stream)
        else:

            def both_sides(side_at, carry, stream=stream):
                product(stream, side_at)
                return carry

            lax.fori_loop(0, n_x, both_sides, 0)
            begin(stream)
    for stream in turns:
        if kinds[stream] == "a":
            product(stream, spot_x)

    def weight_grad(k):
        for part in range(2):
            act_rows[:, part * half : (part + 1) * half] = dot(
                order_ref[...], own_acts[part, k], 1, 1
            ).astype(BF16)
        piece = min(512, width)

        def one(step, carry):
            where = pl.ds(pl.multiple_of(step * piece, piece), piece)
            grad_rows[k, :, where] = jnp.dot(
                act_rows[...], full[k // 2, :, where], preferred_element_type=F32
            ).astype(BF16)
            return carry

        lax.fori_loop(0, width // piece, one, 0)
        pltpu.make_async_copy(grad_rows.at[k], grads.at[0, k], out_sem.at[k]).start()

    def combine(stream, step):
        wait(region(stream, step), halve_recv.at[stream, step])
        for sent in (True, False):

            def add(choice, carry, sent=sent):
                block = block_of(stream, step + 1, choice, sent)
                slot = offset(step) + number(stream, step, choice, sent)
                total = data[stream, block].astype(F32) + recv[stream, slot].astype(F32)
                data[stream, block] = total.astype(BF16)
                if sent:
                    send(stream, step + 1, choice)
                return carry

            lax.fori_loop(0, count(step + 1), add, 0)

    wait_tokens(bits - 1, tok_recv)
    act_copy.wait()
    fill = {(0, 0): 0, (0, 3): 1, (0, 6): 2}
    for step in range(chip_bits - 1):
        for at, stream in enumerate(turns):
            if (step, at) in fill:
                weight_grad(fill[step, at])
            combine(stream, step)

    last = chip_bits - 1
    results = (mixed, token_grad)

    def finish(array, i, keep):
        owner_core = core if keep else 1 - core
        stream = array * per_array + owner_core * (per_array // 2) + i
        wait(recv.at[stream, pl.ds(offset(last), 1)], halve_recv.at[stream, last])
        total = (
            data[stream, chip].astype(F32) + recv[stream, offset(last)].astype(F32)
        ).astype(BF16)
        if keep:
            put(array, i, core, total)
        else:
            data[stream, chip] = total
            remote(
                data.at[stream, chip],
                swap.at[array, i],
                swap_sem.at[0],
                swap_sem.at[1],
                sibling,
            ).start()

    def put(array, i, which, total):
        for part in range(n_x):
            start = pl.multiple_of((part * 2 + which) * quarter, quarter)
            results[array][pl.ds(start, quarter), i * chunk : (i + 1) * chunk] = total[
                part * quarter : (part + 1) * quarter
            ]

    for keep in (False, True):
        for array in range(2):
            for i in range(per_array // 2):
                finish(array, i, keep)
    wait(swap, swap_sem.at[1])
    for array in range(2):
        for i in range(per_array // 2):
            put(array, i, 1 - core, swap[array, i])

    for k in range(3):
        pltpu.make_async_copy(grad_rows.at[k], grads.at[0, k], out_sem.at[k]).wait()
    wait(picked.at[pl.ds(0, n_dp * n_ex - 1)], row_send.at[0])
    wait(relay, relay_send.at[0])
    wait(weights.at[:, my_units, :], fwd_send.at[0])
    for step in range(bits):
        wait_tokens(step, tok_send)
    for step in range(chip_bits):
        for stream in range(len(kinds)):
            wait(region(stream, step), halve_send.at[stream, step])
    wait(swap, swap_sem.at[0])


def fused_step(
    n_dp, n_ex, unit_perm, slab_owner, routes, route_gates, dense_weights, tokens, cotangent
):
    _, block_units, feat = dense_weights.shape
    tok, width = tokens.shape
    share = unit_perm.shape[1] // (n_ex // 2) // n_dp
    pick = share // n_dp
    padded = -(-pick // 16) * 16
    half_units, half = n_dp * padded, n_ex * tok // 2
    blocks, bits, n_x = n_dp * n_ex, log2(n_dp * n_ex), n_dp // 2
    chips, chunk = blocks // 2, 256
    streams = 2 * (width // n_x // chunk)
    any_spec, vmem_spec = pl.BlockSpec(memory_space=pl.ANY), pl.BlockSpec(memory_space=pltpu.VMEM)
    r_rows = tok // 2
    results = pl.pallas_call(
        functools.partial(fused_kernel, n_dp, n_ex),
        out_shape=[
            jax.ShapeDtypeStruct((tok, width // n_dp), BF16),
            jax.ShapeDtypeStruct((tok, width // n_dp), BF16),
            jax.ShapeDtypeStruct((1, 3, share, width), BF16),
        ],
        in_specs=[
            vmem_spec,
            pl.BlockSpec(memory_space=pltpu.SMEM),
            vmem_spec,
            vmem_spec,
            any_spec,
            any_spec,
            any_spec,
        ],
        out_specs=[vmem_spec, vmem_spec, any_spec],
        scratch_shapes=[
            pltpu.VMEM((3, block_units, feat), BF16),
            pltpu.VMEM((2, n_ex * tok, width), BF16),
            pltpu.VMEM((blocks, 3, pick, feat), BF16),
            pltpu.VMEM((3, 2 * half_units, width), BF16),
            pltpu.VMEM((3, half, 2 * half_units), F32),
            pltpu.VMEM((3, half, 2 * half_units), BF16),
            pltpu.VMEM((2, 3, half, half_units), BF16),
            pltpu.VMEM((3, half, half_units), BF16),
            pltpu.VMEM((n_ex, 1, tok), F32),
            pltpu.VMEM((streams, chips, r_rows, chunk), BF16),
            pltpu.VMEM((streams, chips - 1, r_rows, chunk), BF16),
            pltpu.VMEM((2, streams // 4, r_rows, chunk), BF16),
            pltpu.VMEM((n_ex // 2 - 1, 2 * n_dp - 1, 3, pick, feat), BF16),
            pltpu.VMEM((share, share), BF16),
            pltpu.VMEM((share, half_units), BF16),
            pltpu.VMEM((share, n_ex * tok), BF16),
            pltpu.VMEM((3, share, width), BF16),
            pltpu.VMEM((n_ex, 1, tok), F32),
            pltpu.VMEM((half, 128), F32),
            pltpu.VMEM((half, 128), F32),
            pltpu.SemaphoreType.DMA((3,)),
            pltpu.SemaphoreType.DMA((2,)),
            pltpu.SemaphoreType.DMA((1,)),
            pltpu.SemaphoreType.DMA((n_ex,)),
            pltpu.SemaphoreType.DMA((1,)),
            pltpu.SemaphoreType.DMA((n_ex,)),
            pltpu.SemaphoreType.DMA((2, bits)),
            pltpu.SemaphoreType.DMA((2, bits)),
            pltpu.SemaphoreType.DMA((2,)),
            pltpu.SemaphoreType.DMA((streams, bits - 1)),
            pltpu.SemaphoreType.DMA((streams, bits - 1)),
            pltpu.SemaphoreType.DMA((2,)),
            pltpu.SemaphoreType.DMA((3,)),
            pltpu.SemaphoreType.DMA((1,)),
            pltpu.SemaphoreType.DMA((n_ex // 2 - 1, 2 * n_dp - 1)),
        ],
        compiler_params=pltpu.CompilerParams(
            collective_id=2, has_side_effects=True, vmem_limit_bytes=63 << 20
        ),
        name="fused_step",
    )(unit_perm, slab_owner, routes.T, route_gates.T, dense_weights, tokens, cotangent)
    pieces = len(publish_rows(share))
    return pl.pallas_call(
        publish_kernel,
        out_shape=[jax.ShapeDtypeStruct(result.shape, result.dtype) for result in results],
        in_specs=[any_spec] * 3,
        out_specs=[any_spec] * 3,
        scratch_shapes=[
            pltpu.VMEM((2, tok, width // n_dp), BF16),
            pltpu.VMEM((3, share, width), BF16),
            pltpu.SemaphoreType.DMA((2, 3 * pieces + 2)),
        ],
        compiler_params=pltpu.CompilerParams(vmem_limit_bytes=63 << 20),
        name="publish",
    )(*results)


def publish_rows(rows):
    size = -(-rows // 64) * 16
    return [(start, min(size, rows - start)) for start in range(0, rows, size)]


def publish_kernel(mixed, token_grad, grads, mixed_out, token_grad_out, grads_out, small, large, sem):
    moves = [
        (mixed, small.at[0], mixed_out),
        (token_grad, small.at[1], token_grad_out),
    ]
    for k in range(3):
        for start, size in publish_rows(large.shape[1]):
            rows = pl.ds(start, size)
            moves.append((grads.at[0, k, rows], large.at[k, rows], grads_out.at[0, k, rows]))
    for at, (source, middle, _) in enumerate(moves):
        pltpu.make_async_copy(source, middle, sem.at[0, at]).start()
    for at, (source, middle, target) in enumerate(moves):
        pltpu.make_async_copy(source, middle, sem.at[0, at]).wait()
        pltpu.make_async_copy(middle, target, sem.at[1, at]).start()
    for at, (_, middle, target) in enumerate(moves):
        pltpu.make_async_copy(middle, target, sem.at[1, at]).wait()


def gather_plain(n_dp, n_ex, row, picked, tokens, cotangent, table):
    _, pick, wide = picked.shape
    tok, width = tokens.shape
    arrived = lax.all_to_all(picked, ("dp", "expert"), split_axis=0, concat_axis=0, tiled=True)
    arrived = arrived.reshape(n_dp, n_ex, pick, 3, wide // 3)
    weights = jnp.transpose(arrived, (3, 0, 2, 1, 4)).reshape(3, n_dp * pick, width)
    part = width // n_dp
    both = jnp.concatenate(
        [
            lax.dynamic_slice(tokens, (0, row * part), (tok, part)),
            lax.dynamic_slice(cotangent, (0, row * part), (tok, part)),
        ],
        axis=1,
    )
    both = lax.all_gather(both, "expert", axis=0, tiled=True)
    both = lax.all_gather(both, "dp", axis=0, tiled=False)
    all_x = jnp.transpose(both[:, :, :part], (1, 0, 2)).reshape(n_ex * tok, width)
    all_c = jnp.transpose(both[:, :, part:], (1, 0, 2)).reshape(n_ex * tok, width)
    gates = lax.all_to_all(table, "expert", split_axis=0, concat_axis=0, tiled=True)
    return weights, all_x, all_c, gates


def body(dense_weights, tokens, cotangent, routes, route_gates, unit_perm, slab_owner):
    n_dp = lax.axis_size("dp")
    n_ex = lax.axis_size("expert")
    row = lax.axis_index("dp")
    col = lax.axis_index("expert")
    _, block_units, feat = dense_weights.shape
    copies, total_units = unit_perm.shape
    slabs = n_ex // copies
    slab_units = total_units // slabs
    share = slab_units // n_dp
    pick = share // n_dp
    tok, width = tokens.shape

    shares = unit_perm.reshape(n_ex, n_dp, share)
    padded = -(-pick // 16) * 16
    if (
        copies == 2
        and slab_units % 128 == 0
        and pick % 8 == 0
        and feat % 256 == 0
        and n_dp * padded % 128 == 0
        and 2 * n_dp * padded % 256 == 0
        and n_dp == 4
        and n_ex == 8
        and width == n_dp * 512
        and tok == 128
    ):
        return tuple(
            fused_step(
                n_dp,
                n_ex,
                unit_perm,
                slab_owner,
                routes,
                route_gates,
                dense_weights,
                tokens,
                cotangent,
            )
        )
    gate_table = jnp.sum(
        jnp.where(
            routes[None, :, :] == lax.broadcasted_iota(jnp.int32, (n_ex, 1, 1), 0),
            route_gates[None, :, :],
            0.0,
        ),
        axis=2,
    )
    dest = jnp.transpose(shares[slab_owner], (1, 0, 2)).reshape(n_dp * n_ex, share)
    mask, rank = block_ranks(dest // block_units, row)
    place = jnp.where(mask, rank, -1)
    hit = place[:, None, :] == lax.broadcasted_iota(jnp.int32, (1, pick, 1), 1)
    units = jnp.sum(jnp.where(hit, (dest - row * block_units)[:, None, :], 0), axis=2)
    onehot = (
        units.reshape(-1, 1) == lax.broadcasted_iota(jnp.int32, (1, block_units), 1)
    ).astype(BF16)
    side = jnp.concatenate([dense_weights[0], dense_weights[1], dense_weights[2]], axis=1)
    picked = dot(onehot, side, 1, 0).astype(BF16)
    picked = picked.reshape(n_dp * n_ex, pick, 3 * feat)
    mine = lax.dynamic_slice(
        shares, (slab_owner[col], row, 0), (1, 1, share)
    ).reshape(1, share)
    mine_block = mine // block_units
    mask, rank = block_ranks(
        jnp.broadcast_to(mine_block, (n_dp, share)),
        lax.broadcasted_iota(jnp.int32, (n_dp, 1), 0),
    )
    at = jnp.sum(
        jnp.where(mask, rank + lax.broadcasted_iota(jnp.int32, (n_dp, 1), 0) * pick, 0), axis=0
    )
    order = (lax.broadcasted_iota(jnp.int32, (share, share), 1) == at[:, None]).astype(BF16)

    weights, all_x, all_c, gate = gather_plain(
        n_dp, n_ex, row, picked, tokens, cotangent, gate_table
    )
    w_gate, w_up, w_down = weights[0], weights[1], weights[2]
    gate = gate.reshape(n_ex * tok, 1)
    copy_id = slab_owner[col] // slabs
    owner_block = lax.broadcasted_iota(jnp.int32, (n_ex, tok), 0).reshape(n_ex * tok, 1)
    both_weight = gate + (owner_block * copies // n_ex == copy_id).astype(F32)

    pre_gate = dot(all_x, w_gate, 1, 1)
    pre_up = dot(all_x, w_up, 1, 1)
    d_hidden = dot(all_c, w_down, 1, 1)
    act, slope = silu_parts(pre_gate)
    hidden = act * pre_up
    d_gate = d_hidden * pre_up * slope
    d_up = d_hidden * act

    out = dot((both_weight * hidden).astype(BF16), w_down, 1, 0).astype(BF16)
    back = (
        dot((both_weight * d_gate).astype(BF16), w_gate, 1, 0)
        + dot((both_weight * d_up).astype(BF16), w_up, 1, 0)
    ).astype(BF16)

    acts = [(gate * values).astype(BF16) for values in (d_gate, d_up, hidden)]
    if out.size * out.dtype.itemsize <= 1 << 23:
        mixed, token_grad, weight_grads = halving_sum(
            n_dp, n_ex, [out, back], acts + [order], [all_x, all_c]
        )
    else:
        acts = [dot(order, values, 1, 1).astype(BF16) for values in acts]
        weight_grads = jnp.stack(
            [dot(acts[0], all_x, 1, 0), dot(acts[1], all_x, 1, 0), dot(acts[2], all_c, 1, 0)]
        ).astype(BF16)[None]
        (mixed,) = halving_sum(n_dp, n_ex, [out])
        (token_grad,) = halving_sum(n_dp, n_ex, [back])
    return (mixed, token_grad, weight_grads)


def solution(mesh):
    in_specs = (
        P(None, "dp", "expert"),
        P("expert", None),
        P("expert", None),
        P("expert", None),
        P("expert", None),
        P(),
        P(),
    )
    out_specs = (P("expert", "dp"), P("expert", "dp"), P("expert", None, "dp", None))
    return jax.shard_map(body, mesh=mesh, in_specs=in_specs, out_specs=out_specs, check_vma=False)
```
